256 devices in a mesh: dp: 128 (over x, z, y_hi, core), shard: 2 (over y_lo).
Axes of the slice: x: 4, y: 4 (y_hi: 2, y_lo: 2; y = y_hi * 2 + y_lo), z: 8, core: 2. Of those that a mesh axis runs over, the one named last changes fastest.
Arguments:
- clips: bfloat16 [512, 5, 256, 512], P(('dp', 'shard')), may hold values from -16 to 16
- code_grad: bfloat16 [512, 5, 256, 18], P(('dp', 'shard')), may hold values from -6 to 6
- conv_weight: bfloat16 [1536, 512], replicated, may hold values from -0.15625 to 0.15625
- norm_gain: float32 [512], replicated, may hold values from 0.5 to 1.5
- proj_weight: bfloat16 [512, 18], replicated, may hold values from -0.25 to 0.25
- code_bias: float32 [18], replicated, may hold values from -1 to 1
- rotation: float32 [18, 18], replicated, may hold values from -1.5 to 1.5
- first_moment: float32 [1536, 512], P('shard'), may hold values from -4 to 4
- second_moment: float32 [1536, 512], P('shard'), may hold values from 0.01 to 0.3
Outputs:
- new_weight: bfloat16 [1536, 512], replicated
- first_moment_out: float32 [1536, 512], P('shard')
- second_moment_out: float32 [1536, 512], P('shard')
- input_grad: bfloat16 [512, 5, 256, 512], P(('dp', 'shard'))
- loss: float32 [], replicated
The draws below stay inside these ranges and needn't reach their ends.
All inputs are finite; a program needn't handle non-finite values.
Results may differ from the reference program's by a relative error of at most 0.014.
Values may be sent and summed in bfloat16 or wider, within the bound.
No kernel may reach another device: no remote copies, remote signals or barrier semaphores. Data moves between devices by JAX's collectives and lax.ppermute only.
A program may use at most 128 MiB of HBM per device.

```python
import math
import jax
import jax.numpy as jnp
from jax import lax

C = 512
BITS = 18
FRAMES = 5
SITES = 256
CLIP_DEV = 2
CLIPS = 512


def draw_clips(key, part):
    block_count = CLIPS // CLIP_DEV
    jitter_key = jax.random.fold_in(key, 11)
    offset_key = jax.random.fold_in(key, 23)
    spike_key = jax.random.fold_in(key, 37)
    extent = (CLIPS, FRAMES, SITES, C)
    jitter = jnp.clip(jax.random.normal(jitter_key, extent, jnp.float32), -4.0, 4.0)
    offset = jnp.clip(1.5 * jax.random.normal(offset_key, (block_count, C), jnp.float32), -4.5, 4.5)
    chosen = jax.random.randint(spike_key, (block_count, 1), 0, C)
    factor = jnp.where(jnp.arange(C)[None, :] == chosen, 4.0, 1.0).astype(jnp.float32)
    offset = jnp.repeat(offset, CLIP_DEV, axis=0)
    factor = jnp.repeat(factor, CLIP_DEV, axis=0)
    values = jitter * factor[:, None, None, :] + offset[:, None, None, :]
    return jnp.clip(values, -16.0, 16.0).astype(jnp.bfloat16)


def steps_of(own_key, dims, cuts, smallest, high):
    def one(dim, blocks):
        steps = jax.random.uniform(jax.random.fold_in(jax.random.fold_in(own_key, 6), dim), (blocks,), jnp.float32, smallest / len(cuts), high / len(cuts))
        return jnp.repeat(jnp.exp(steps), dims[dim] // blocks).reshape((-1,) + (1,) * (len(dims) - dim - 1))

    level = one(*cuts[0])
    for cut in cuts[1:]:
        level = level * one(*cut)
    return level


def bell_draw(rng, shape, spread, reach, shards=(), dtype=jnp.bfloat16):
    factor_of = steps_of(rng, shape, shards, -0.22, 0.18) if shards else 1.0
    drawn = jax.random.normal(rng, shape, jnp.float32) * spread * factor_of
    return jnp.minimum(jnp.maximum(drawn, -reach), reach).astype(dtype)


def setup_inputs(seed: int = 0) -> dict:
    seeds = jax.random.split(jax.random.key(seed), 10)
    return {
        "clips": draw_clips(jax.random.fold_in(seeds[9], 71), 0),
        "code_grad": bell_draw(seeds[1], (CLIPS, FRAMES, SITES, BITS), 1.0, 6.0, ((0, 256),)),
        "conv_weight": bell_draw(seeds[2], (3 * C, C), (3 * C) ** -0.5, 0.15625),
        "norm_gain": jnp.clip(1.0 + 0.1 * jax.random.normal(seeds[3], (C,), jnp.float32), 0.5, 1.5),
        "proj_weight": bell_draw(seeds[4], (C, BITS), C ** -0.5, 0.25),
        "code_bias": jnp.clip(jax.random.uniform(seeds[5], (BITS,), jnp.float32, -1.0, 1.0), -1.0, 1.0),
        "rotation": bell_draw(seeds[6], (BITS, BITS), BITS ** -0.5, 1.5, (), jnp.float32),
        "first_moment": bell_draw(seeds[7], (3 * C, C), 0.3, 4.0, ((0, 2),), jnp.float32),
        "second_moment": jnp.clip(jnp.exp(math.log(0.3) - 3.4011974 * jax.random.uniform(seeds[8], (3 * C, C), jnp.float32) ** steps_of(seeds[8], (3 * C, C), ((0, 2),), -0.2, 0.2)), 0.01, 0.3),
    }


def stacked_taps(block):
    batch, frames, sites, width = block.shape
    padded = jnp.pad(block, ((0, 0), (2, 0), (0, 0), (0, 0)))
    taps = [padded[:, 2 - k:2 - k + frames] for k in range(3)]
    return jnp.concatenate(taps, axis=3).reshape(batch * frames * sites, 3 * width)

def forward(block, conv_weight, norm_gain, proj_weight, code_bias, rotation):
    width = block.shape[3]
    stacked = stacked_taps(block)
    hidden = block.reshape(-1, width).astype(jnp.float32) + jnp.dot(stacked, conv_weight, preferred_element_type=jnp.float32)
    inverse = lax.rsqrt(lax.optimization_barrier(jnp.mean(hidden * hidden, axis=1, keepdims=True)) + 1e-06)
    unit = hidden * inverse
    normed = (unit * norm_gain).astype(jnp.bfloat16)
    latent = jnp.dot(normed, proj_weight, preferred_element_type=jnp.float32) + code_bias
    rotated = jnp.dot(latent, rotation, precision=lax.Precision.HIGHEST)
    codes = jnp.tanh(rotated)
    return (stacked, inverse, unit, rotated, codes)

def token_terms(rotated, codes, cotangent):
    probs = (1.0 + codes) / 2.0
    logit = 2.0 * rotated
    entropy = jax.nn.softplus(logit) - logit * probs
    token_loss = cotangent * codes + 0.25 * (rotated - codes) ** 2 + 0.1 * entropy
    return (probs, logit, jnp.sum(token_loss))

def backward(block, cotangent, conv_weight, norm_gain, proj_weight, rotation, saved, lean, clip_count):
    stacked, inverse, unit, rotated, codes = saved
    probs = (1.0 + codes) / 2.0
    logit = 2.0 * rotated
    slope = 1.0 - codes * codes
    d_rot = (cotangent * slope + 0.5 * (rotated - codes) * (1.0 - slope) - 0.2 * logit * probs * (1.0 - probs) - 0.05 * slope * lean) / clip_count
    d_lat = jnp.dot(d_rot, rotation.T, precision=lax.Precision.HIGHEST)
    d_norm = jnp.dot(d_lat, proj_weight.astype(jnp.float32).T, precision=lax.Precision.HIGHEST)
    scaled = d_norm * norm_gain
    d_hidden = inverse * (scaled - unit * lax.optimization_barrier(jnp.mean(scaled * unit, axis=1, keepdims=True)))
    d_conv = d_hidden.astype(jnp.bfloat16)
    batch, frames, sites, width = block.shape
    d_taps = lax.dot_general(d_conv, conv_weight, (((1,), (1,)), ((), ())), preferred_element_type=jnp.float32)
    d_taps = d_taps.reshape(batch, frames, sites, 3, width)
    padded = jnp.pad(d_taps, ((0, 0), (0, 2), (0, 0), (0, 0), (0, 0)))
    back = padded[:, 0:frames, :, 0, :] + padded[:, 1:frames + 1, :, 1, :] + padded[:, 2:frames + 2, :, 2, :]
    input_grad = (d_hidden.reshape(batch, frames, sites, width) + back).astype(jnp.bfloat16)
    return (stacked, d_conv, input_grad)

def reference(clips, code_grad, conv_weight, norm_gain, proj_weight, code_bias, rotation, first_moment, second_moment):
    clip_count = clips.shape[0]
    token_count = clips.shape[0] * clips.shape[1] * clips.shape[2]
    bit_count = code_grad.shape[3]

    def stats_step(carry, item):
        block, cotangent = item
        saved = forward(block[None], conv_weight, norm_gain, proj_weight, code_bias, rotation)
        probs, logit, loss_part = token_terms(saved[3], saved[4], cotangent.reshape(-1, bit_count).astype(jnp.float32))
        return ((carry[0] + lax.optimization_barrier(jnp.sum(probs, axis=0)), carry[1] + loss_part), None)
    init = (jnp.zeros((bit_count,), jnp.float32), jnp.zeros((), jnp.float32))
    (bit_total, loss_total), _ = lax.scan(stats_step, init, (clips, code_grad))
    bit_mean = bit_total / token_count
    code_entropy = jnp.sum(-bit_mean * jnp.log(bit_mean) - (1.0 - bit_mean) * jnp.log(1.0 - bit_mean))
    loss = loss_total / token_count - 0.1 * code_entropy
    lean = jnp.log((1.0 - bit_mean) / bit_mean)

    def grad_step(carry, item):
        block, cotangent = item
        saved = forward(block[None], conv_weight, norm_gain, proj_weight, code_bias, rotation)
        stacked, d_conv, input_grad = backward(block[None], cotangent.reshape(-1, bit_count).astype(jnp.float32), conv_weight, norm_gain, proj_weight, rotation, saved, lean, clip_count)
        term = lax.dot_general(stacked, d_conv, (((0,), (0,)), ((), ())), preferred_element_type=jnp.float32)
        return (carry + term, input_grad[0])
    grad, input_grad = lax.scan(grad_step, jnp.zeros(conv_weight.shape, jnp.float32), (clips, code_grad))
    first_out = 0.9 * first_moment + 0.1 * grad
    second_out = 0.99 * second_moment + 0.01 * grad * grad
    new_weight = (conv_weight.astype(jnp.float32) - 0.001 * first_out / (jnp.sqrt(second_out) + 1e-08)).astype(jnp.bfloat16)
    return (new_weight, first_out, second_out, input_grad, loss)
```

```python
import functools

import jax
import jax.numpy as jnp
from jax import lax
from jax.experimental import pallas as pl
from jax.experimental.pallas import tpu as pltpu
from jax.sharding import Mesh
from jax.sharding import PartitionSpec as P

ALL = ("x", "z", "yh", "core", "yl")
PLANE = ("x", "yh", "yl")
ROWS = 24
LANES = 128
F32 = jnp.float32
BF16 = jnp.bfloat16
NT = (((1,), (1,)), ((), ()))
TN = (((0,), (0,)), ((), ()))
EXACT = lax.Precision.HIGHEST


def hi_lo(value):
    high = value.astype(BF16)
    return high, (value - high.astype(F32)).astype(BF16)


def diagonal(row, count):
    grid = jnp.broadcast_to(row, (count, row.shape[1]))
    at = lax.broadcasted_iota(jnp.int32, grid.shape, 0)
    to = lax.broadcasted_iota(jnp.int32, grid.shape, 1)
    return jnp.sum(jnp.where(at == to, grid, 0.0), axis=1, keepdims=True)


def lane_groups(value):
    part = value[:, :LANES]
    for g in range(1, value.shape[1] // LANES):
        part = part + value[:, g * LANES : (g + 1) * LANES]
    return part


def forward_kernel(
    x_ref, w_ref, proj_ref, gain_ref, code_bias_ref, rotation_ref, cg_ref,
    h_ref, xt_ref, base_ref, slope_ref, q_ref, ag_out, stat_ref,
    map_ref, bias_ref, ag_ref, sum_ref,
):
    clip = pl.program_id(0)
    frames, sites, width = x_ref.shape[1:]
    bits = rotation_ref.shape[0]

    @pl.when(clip == 0)
    def _():
        map_ref[...] = jnp.zeros_like(map_ref)
        bias_ref[...] = jnp.zeros_like(bias_ref)
        map_ref[:bits, :] = (
            lax.dot_general(
                rotation_ref[...], proj_ref[...].astype(F32), TN, precision=EXACT, preferred_element_type=F32
            )
            * gain_ref[...]
        )
        row = jnp.dot(code_bias_ref[...], rotation_ref[...], precision=EXACT, preferred_element_type=F32)
        bias_ref[:bits, :] = jnp.broadcast_to(diagonal(row, bits), (bits, LANES))
        high, low = hi_lo(map_ref[...])
        ag_ref[...] = jnp.concatenate([high, low], axis=0)
        ag_out[...] = ag_ref[...]
        sum_ref[...] = jnp.zeros_like(sum_ref)

    ones = jnp.ones((8, LANES), F32)
    bias = bias_ref[:, :1]
    total_p = jnp.zeros((ROWS, LANES), F32)
    total_l = jnp.zeros((ROWS, LANES), F32)
    for f in range(frames):
        taps = min(f, 2) + 1
        block = x_ref[0, f]
        stacked = jnp.concatenate([x_ref[0, f - k] for k in range(taps)], axis=1)
        hidden = block.astype(F32) + jnp.dot(
            stacked, w_ref[: taps * width, :], preferred_element_type=F32
        )
        rounded = hidden.astype(BF16)
        h_ref[0, f] = rounded
        xt_ref[0, :, f * sites : (f + 1) * sites] = block.T
        mean = (
            lax.dot_general(ones, lane_groups(hidden * hidden), NT, preferred_element_type=F32)[:1] / width
        )
        inv = lax.rsqrt(mean + 1e-06)
        both = lax.dot_general(ag_ref[...], rounded, NT, preferred_element_type=F32)
        raw = both[:ROWS] + both[ROWS:]
        rotated = raw * inv + bias
        cotangent = cg_ref[0, f].astype(F32)
        small = jnp.exp(-2.0 * jnp.abs(rotated))
        size = (1.0 - small) / (1.0 + small)
        codes = jnp.where(rotated < 0.0, -size, size)
        probs = 0.5 + 0.5 * codes
        logit = 2.0 * rotated
        gap = rotated - codes
        entropy = jnp.maximum(logit, 0.0) + jnp.log(1.0 + small) - logit * probs
        total_p = total_p + lane_groups(probs)
        total_l = total_l + lane_groups(cotangent * codes + 0.25 * gap * gap + 0.1 * entropy)
        slope = 1.0 - codes * codes
        base = cotangent * slope + 0.5 * gap * (1.0 - slope) - 0.1 * rotated * slope
        base_ref[0, f] = base * inv
        slope_ref[0, f] = slope * inv
        q_ref[0, f] = raw * (inv * inv) / width
    sum_ref[:ROWS] += total_p
    sum_ref[ROWS:] += total_l

    @pl.when(clip == pl.num_programs(0) - 1)
    def _():
        ones = jnp.ones((8, LANES), F32)
        probs = sum_ref[:ROWS]
        at = lax.broadcasted_iota(jnp.int32, probs.shape, 0)
        losses = jnp.sum(jnp.where(at < bits, sum_ref[ROWS:], 0.0), axis=0, keepdims=True)
        table = jnp.where(at < bits, probs, jnp.where(at == bits, losses, 0.0))
        filled = jnp.concatenate([table, jnp.zeros((LANES - ROWS, LANES), F32)], axis=0)
        row = lax.dot_general(ones, filled, NT, precision=EXACT, preferred_element_type=F32)
        stat_ref[...] = row[:1]


def backward_kernel(
    bits, clip_count, token_count, core_ref,
    h_ref, xt_ref, base_ref, slope_ref, q_ref, ag_ref, part_ref,
    d_ref, mine_ref, theirs_ref, loss_ref,
    acc_ref, lean_ref, right_ref,
):
    clip = pl.program_id(0)
    frames, sites, width = h_ref.shape[1:]

    @pl.when(clip == 0)
    def _():
        total = jnp.sum(part_ref[...], axis=0, keepdims=True)
        lane = lax.broadcasted_iota(jnp.int32, total.shape, 1)
        mean = jnp.where(lane < bits, total / token_count, 0.5)
        lean = jnp.log((1.0 - mean) / mean)
        entropy = -mean * jnp.log(mean) - (1.0 - mean) * jnp.log(1.0 - mean)
        term = jnp.where(
            lane < bits, -0.1 * entropy, jnp.where(lane == bits, total / token_count, 0.0)
        )
        loss_ref[...] = jnp.sum(term, axis=1, keepdims=True)
        lean_ref[...] = jnp.broadcast_to(diagonal(lean, ROWS) * 0.05, (ROWS, LANES))
        high = ag_ref[:ROWS]
        low = ag_ref[ROWS:]
        right_ref[:, :width] = jnp.concatenate(
            [high, high, low, jnp.zeros((LANES - 3 * ROWS, width), BF16)], axis=0
        )
        at = lax.broadcasted_iota(jnp.int32, (LANES, LANES), 0)
        right_ref[:, width:] = jnp.where((at >= 3 * ROWS) & (at < 5 * ROWS), 1.0, 0.0).astype(BF16)

    lean = lean_ref[:, :1]
    for f in range(frames):
        u = (base_ref[0, f] - slope_ref[0, f] * lean) * (1.0 / clip_count)
        u_hi, u_lo = hi_lo(u)
        q_hi, q_lo = hi_lo(u * q_ref[0, f])
        spare = jnp.zeros((LANES - 5 * ROWS, sites), BF16)
        left = jnp.concatenate([u_hi, u_lo, u_hi, q_hi, q_lo, spare], axis=0)
        out = lax.dot_general(left, right_ref[...], TN, preferred_element_type=F32)
        centre = jnp.concatenate([out[:, width:]] * (width // LANES), axis=1)
        d_hidden = out[:, :width] - centre * h_ref[0, f].astype(F32)
        d_ref[0, f] = d_hidden.astype(BF16)

    def store(target, column, k, total):
        block = target.shape[1]
        for piece in range(3 * width // block):
            start = piece * block - k * width
            low, high = max(start, 0), min(start + block, width)
            if low >= high:
                continue
            half, quarter = divmod(piece, 4)
            slot = column * 8 + quarter * 2 + half
            target[slot, low - start : high - start, :] = total[low:high]

    for k in range(3):
        count = (frames - k) * sites
        d_part = d_ref[0, k:].reshape(count, width)
        part = jnp.dot(xt_ref[0, :, :count], d_part, preferred_element_type=F32)
        rows = pl.ds(k * width, width)

        @pl.when(clip == 0)
        def _():
            acc_ref[rows, :] = part

        @pl.when(clip != 0)
        def _():
            total = (acc_ref[rows, :] + part).astype(BF16)
            pieces = [total[:, g * LANES : (g + 1) * LANES] for g in range(width // LANES)]

            @pl.when(core_ref[0] == 0)
            def _():
                for c in range(2):
                    store(mine_ref, c, k, pieces[c])
                    store(theirs_ref, c, k, pieces[2 + c])

            @pl.when(core_ref[0] != 0)
            def _():
                for c in range(2):
                    store(mine_ref, c, k, pieces[2 + c])
                    store(theirs_ref, c, k, pieces[c])


def input_kernel(d_ref, w_ref, out_ref):
    frames, sites, width = d_ref.shape[1:]
    for f in range(frames):
        total = d_ref[0, f].astype(F32)
        for k in range(min(3, frames - f)):
            total = total + lax.dot_general(
                d_ref[0, f + k], w_ref[k * width : (k + 1) * width, :], NT, preferred_element_type=F32
            )
        out_ref[0, f] = total.astype(BF16)


def updated(weight, first, second, grad):
    first_out = 0.9 * first + 0.1 * grad
    second_out = 0.99 * second + 0.01 * grad * grad
    new = (weight - 0.001 * first_out / (jnp.sqrt(second_out) + 1e-08)).astype(BF16)
    return new, first_out, second_out


def block_kernel(place_ref, parts_ref, w_ref, m_ref, v_ref, send_ref):
    grad = jnp.sum(parts_ref[...].astype(F32), axis=0).astype(BF16)
    new, _, _ = updated(w_ref[...].astype(F32), m_ref[...], v_ref[...], grad.astype(F32))
    for half in range(2):

        @pl.when(place_ref[0] == half)
        def _():
            for d in range(send_ref.shape[0]):
                send_ref[d] = grad if d % 2 == half else new


def final_kernel(place_ref, near_ref, far_ref, w_ref, m_ref, v_ref, new_ref, first_ref, second_ref):
    step = pl.program_id(0)
    rows = m_ref.shape[0]
    block = near_ref.shape[1]

    def write(source, half):
        for quarter in range(rows // block):
            part = pl.ds(quarter * block, block)
            here = pl.ds(half * rows + quarter * block, block)
            there = pl.ds((1 - half) * rows + quarter * block, block)
            grad = source[quarter * 2 + half].astype(F32)
            new, first_out, second_out = updated(w_ref[here, :].astype(F32), m_ref[part, :], v_ref[part, :], grad)
            new_ref[here, :] = new
            first_ref[part, :] = first_out
            second_ref[part, :] = second_out
            new_ref[there, :] = source[quarter * 2 + 1 - half]

    near = (step // 2) == place_ref[1]
    for half in range(2):

        @pl.when((place_ref[0] == half) & near)
        def _():
            write(near_ref, half)

        @pl.when((place_ref[0] == half) & jnp.logical_not(near))
        def _():
            write(far_ref, half)


def per_clip(shape):
    return pl.BlockSpec((1, *shape[1:]), lambda c, *_: (c,) + (0,) * (len(shape) - 1))


def whole(shape):
    return pl.BlockSpec(shape, lambda *_: (0,) * len(shape))


def shaped(outs):
    return [jax.ShapeDtypeStruct(s, t) for s, t in outs]


def run_forward(clips, weight, proj, gain, code_bias, rotation, cotangent):
    batch, frames, sites, width = clips.shape
    rows = (batch, frames, ROWS, sites)
    outs = [
        (clips.shape, BF16), ((batch, width, frames * sites), BF16),
        (rows, F32), (rows, F32), (rows, F32), ((2 * ROWS, width), BF16), ((1, LANES), F32),
    ]
    shared = (weight, proj, gain, code_bias, rotation)
    return pl.pallas_call(
        forward_kernel,
        grid=(batch,),
        in_specs=[per_clip(clips.shape)] + [whole(a.shape) for a in shared] + [per_clip(cotangent.shape)],
        out_specs=[per_clip(s) for s, _ in outs[:5]] + [whole(s) for s, _ in outs[5:]],
        out_shape=shaped(outs),
        scratch_shapes=[
            pltpu.VMEM((ROWS, width), F32), pltpu.VMEM((ROWS, LANES), F32),
            pltpu.VMEM((2 * ROWS, width), BF16), pltpu.VMEM((2 * ROWS, LANES), F32),
        ],
        name="forward",
    )(clips, *shared, cotangent)


def run_backward(bits, clip_count, token_count, core, saved, ag, parts, row_count):
    hidden = saved[0]
    batch, frames, sites, width = hidden.shape
    block = (16, row_count // 8, LANES)
    outs = [(hidden.shape, BF16), (block, BF16), (block, BF16), ((1, 1), F32)]
    return pl.pallas_call(
        functools.partial(backward_kernel, bits, clip_count, token_count),
        grid_spec=pltpu.PrefetchScalarGridSpec(
            num_scalar_prefetch=1,
            grid=(batch,),
            in_specs=[per_clip(a.shape) for a in saved] + [whole(ag.shape), whole(parts.shape)],
            out_specs=[per_clip(hidden.shape)] + [whole(s) for s, _ in outs[1:]],
            scratch_shapes=[
                pltpu.VMEM((row_count, width), F32), pltpu.VMEM((ROWS, LANES), F32),
                pltpu.VMEM((LANES, width + LANES), BF16),
            ],
        ),
        out_shape=shaped(outs),
        name="backward",
    )(core, *saved, ag, parts)


def run_input(d_conv, weight):
    return pl.pallas_call(
        input_kernel,
        grid=(d_conv.shape[0],),
        in_specs=[per_clip(d_conv.shape), whole(weight.shape)],
        out_specs=per_clip(d_conv.shape),
        out_shape=jax.ShapeDtypeStruct(d_conv.shape, BF16),
        name="input_grad",
    )(d_conv, weight)


def run_block(place, parts, weight, first, second):
    block = parts.shape[1:]
    send = (16, *block)
    return pl.pallas_call(
        block_kernel,
        grid_spec=pltpu.PrefetchScalarGridSpec(
            num_scalar_prefetch=1,
            grid=(1,),
            in_specs=[
                whole(parts.shape),
                pl.BlockSpec(block, lambda i, p: (p[0] * 4 + p[2], p[3])),
                pl.BlockSpec(block, lambda i, p: (p[2], p[3])),
                pl.BlockSpec(block, lambda i, p: (p[2], p[3])),
            ],
            out_specs=whole(send),
        ),
        out_shape=jax.ShapeDtypeStruct(send, BF16),
        name="owner_step",
    )(place, parts, weight, first, second)


def run_final(place, near, far, weight, first, second):
    total, width = weight.shape
    owned = first.shape[0]
    side = near.shape[0] // 2
    column = lambda rows: pl.BlockSpec((rows, LANES), lambda i, p: (0, i))
    part = pl.BlockSpec((side, *near.shape[1:]), lambda i, p: (i % 2, 0, 0))
    return pl.pallas_call(
        final_kernel,
        grid_spec=pltpu.PrefetchScalarGridSpec(
            num_scalar_prefetch=1,
            grid=(width // LANES,),
            in_specs=[part, part, column(total), column(owned), column(owned)],
            out_specs=[column(total), column(owned), column(owned)],
        ),
        out_shape=shaped([((total, width), BF16), ((owned, width), F32), ((owned, width), F32)]),
        name="final_step",
    )(place, near, far, weight, first, second)


def spread(value, axes):
    return lax.all_to_all(value, axes, 0, 0, tiled=True)


def swapped(value):
    return lax.ppermute(value, "core", [(0, 1), (1, 0)])


def on_device(clips, code_grad, conv_weight, norm_gain, proj_weight, code_bias, rotation, first_moment, second_moment):
    bits = code_grad.shape[3]
    devices = lax.axis_size(ALL)
    batch, frames, sites, width = clips.shape
    clip_count = batch * devices
    token_count = clip_count * frames * sites
    half, core = lax.axis_index("yl"), lax.axis_index("core")
    x_at, y_at = lax.axis_index("x"), lax.axis_index("yh")
    place = jnp.stack([half, core, (x_at % 2) * 2 + y_at, core * 2 + x_at // 2]).astype(jnp.int32)
    cotangent = jnp.pad(code_grad.transpose(0, 1, 3, 2), ((0, 0), (0, 0), (0, ROWS - bits), (0, 0)))
    *saved, ag, stats = run_forward(
        clips, conv_weight, proj_weight.T, norm_gain[None, :], code_bias[None, :], rotation, cotangent
    )
    parts = spread(jnp.broadcast_to(stats, (devices, LANES)), ALL)
    d_conv, mine, theirs, loss = run_backward(
        bits, clip_count, token_count, place[1:2], saved, ag, parts, conv_weight.shape[0]
    )
    chip = (mine.astype(F32) + swapped(theirs).astype(F32)).astype(BF16)
    plane = spread(chip, PLANE)
    input_grad = run_input(d_conv, conv_weight)
    column = jnp.sum(plane.astype(F32), axis=0).astype(BF16)
    tower = spread(jnp.broadcast_to(column, (lax.axis_size("z"), *column.shape)), "z")
    near = spread(run_block(place, tower, conv_weight, first_moment, second_moment), PLANE)
    far = swapped(near)
    new_weight, first_out, second_out = run_final(place, near, far, conv_weight, first_moment, second_moment)
    return new_weight, first_out, second_out, input_grad, loss[0, 0]


def solution(mesh):
    finer = Mesh(mesh.devices.reshape(4, 8, 2, 2, mesh.shape["shard"]), ALL)
    split = P(ALL, None, None, None)
    in_specs = (split, split, P(), P(), P(), P(), P(), P("yl", None), P("yl", None))
    out_specs = (P(), P("yl", None), P("yl", None), split, P())
    return jax.shard_map(on_device, mesh=finer, in_specs=in_specs, out_specs=out_specs, check_vma=False)
```

```python
import functools

import jax
import jax.numpy as jnp
from jax import lax
from jax.experimental import pallas as pl
from jax.experimental.pallas import tpu as pltpu
from jax.sharding import Mesh
from jax.sharding import PartitionSpec as P

ALL = ("x", "z", "yh", "core", "yl")
PLANE = ("x", "yh", "yl")
ROWS = 24
ROW_STEP = 512
COL_STEP = 512
GRAD_STEP = 512
LANES = 128
F32 = jnp.float32
BF16 = jnp.bfloat16
NT = (((1,), (1,)), ((), ()))
TN = (((0,), (0,)), ((), ()))
EXACT = lax.Precision.HIGHEST


def hi_lo(value):
    high = value.astype(BF16)
    return high, (value - high.astype(F32)).astype(BF16)


def diagonal(row, count):
    grid = jnp.broadcast_to(row, (count, row.shape[1]))
    at = lax.broadcasted_iota(jnp.int32, grid.shape, 0)
    to = lax.broadcasted_iota(jnp.int32, grid.shape, 1)
    return jnp.sum(jnp.where(at == to, grid, 0.0), axis=1, keepdims=True)


def lane_groups(value):
    part = value[:, :LANES]
    for g in range(1, value.shape[1] // LANES):
        part = part + value[:, g * LANES : (g + 1) * LANES]
    return part


def copy(source, target, sem):
    return pltpu.make_async_copy(source, target, sem)


def forward_kernel(
    _, x_hbm, w_hbm, proj_hbm, gain_hbm, code_bias_hbm, rotation_hbm, cg_hbm,
    h_ref, xt_hbm, base_ref, slope_ref, q_ref, ag_ref, stat_ref,
    x_ref, w_ref, map_ref, cot_ref, xt_ref, proj_ref, gain_ref, code_bias_ref, rotation_ref, cg_ref,
    x_sem, w_sem, xt_sem, small_sem,
):
    batch, frames, sites, width = x_hbm.shape
    bits = rotation_ref.shape[0]
    tokens = batch * sites
    pairs = [
        (proj_hbm, proj_ref), (gain_hbm, gain_ref), (code_bias_hbm, code_bias_ref),
        (rotation_hbm, rotation_ref), (cg_hbm, cg_ref),
    ]
    small_copies = [copy(a, b, small_sem.at[i]) for i, (a, b) in enumerate(pairs)]
    for one in small_copies:
        one.start()
    x_copies = [
        [copy(x_hbm.at[c, f], x_ref.at[f, pl.ds(c * sites, sites)], x_sem.at[f, c]) for c in range(batch)]
        for f in range(frames)
    ]
    w_copies = [
        copy(w_hbm.at[pl.ds(k * width, width)], w_ref.at[pl.ds(k * width, width)], w_sem.at[k]) for k in range(3)
    ]
    for f in range(frames):
        for one in x_copies[f]:
            one.start()
        if f < 3:
            w_copies[f].start()
    map_ref[...] = jnp.zeros_like(map_ref)
    cot_ref[...] = jnp.zeros_like(cot_ref)
    for one in small_copies:
        one.wait()
    map_ref[:bits, :] = (
        lax.dot_general(
            rotation_ref[...], proj_ref[...].astype(F32), TN, precision=EXACT, preferred_element_type=F32
        )
        * gain_ref[...]
    )
    row = jnp.dot(code_bias_ref[...], rotation_ref[...], precision=EXACT, preferred_element_type=F32)
    bias = diagonal(jnp.concatenate([row, jnp.zeros((1, LANES - bits), F32)], axis=1), ROWS)
    high, low = hi_lo(map_ref[...])
    ag_ref[...] = jnp.concatenate([high, low], axis=0)
    ones = jnp.ones((8, LANES), F32)
    total_p = jnp.zeros((ROWS, LANES), F32)
    total_l = jnp.zeros((ROWS, LANES), F32)
    def multiply(f):
        means = []
        for start in range(0, tokens, ROW_STEP):
            rows = slice(start, start + ROW_STEP)
            part = jnp.zeros((ROW_STEP, LANES), F32)
            for first in range(0, width, COL_STEP):
                cols = slice(first, first + COL_STEP)
                hidden = x_ref[f, rows, cols].astype(F32)
                for k in range(min(f, 2) + 1):
                    hidden = hidden + jnp.dot(
                        x_ref[f - k, rows, :], w_ref[k * width : (k + 1) * width, cols], preferred_element_type=F32
                    )
                h_ref[f, rows, cols] = hidden.astype(BF16)
                part = part + lane_groups(hidden * hidden)
            means.append(lax.dot_general(ones, part, NT, preferred_element_type=F32)[:1] / width)
        both = lax.dot_general(ag_ref[...], h_ref[f], NT, preferred_element_type=F32)
        return jnp.concatenate(means, axis=1), both[:ROWS] + both[ROWS:]

    def decide(f, mean, raw):
        inv = lax.rsqrt(mean + 1e-06)
        rotated = raw * inv + bias
        cot_ref[f, :bits, :sites] = cg_ref[f, :, 0, :].astype(F32)
        cot_ref[f, :bits, sites:] = cg_ref[f, :, 1, :].astype(F32)
        cotangent = cot_ref[f]
        small = jnp.exp(-2.0 * jnp.abs(rotated))
        size = (1.0 - small) / (1.0 + small)
        codes = jnp.where(rotated < 0.0, -size, size)
        probs = 0.5 + 0.5 * codes
        logit = 2.0 * rotated
        gap = rotated - codes
        entropy = jnp.maximum(logit, 0.0) + jnp.log(1.0 + small) - logit * probs
        slope = 1.0 - codes * codes
        base = cotangent * slope + 0.5 * gap * (1.0 - slope) - 0.1 * rotated * slope
        base_ref[f] = base * inv
        slope_ref[f] = slope * inv
        q_ref[f] = raw * (inv * inv) / width
        xt_ref[:, f * tokens : (f + 1) * tokens] = x_ref[f].T
        return lane_groups(probs), lane_groups(cotangent * codes + 0.25 * gap * gap + 0.1 * entropy)

    def arrive(f):
        for one in x_copies[f]:
            one.wait()
        if f < 3:
            w_copies[f].wait()

    waiting = []
    for f in range(frames):
        arrive(f)
        ready = multiply(f)
        for earlier in waiting:
            sums = decide(*earlier)
            total_p = total_p + sums[0]
            total_l = total_l + sums[1]
        waiting = [(f, *ready)]
    span = pl.ds(0, (frames - 1) * tokens)
    first_part = copy(xt_ref.at[:, span], xt_hbm.at[:, span], xt_sem.at[0])
    first_part.start()
    sums = decide(*waiting[0])
    total_p = total_p + sums[0]
    total_l = total_l + sums[1]
    span = pl.ds((frames - 1) * tokens, tokens)
    last_part = copy(xt_ref.at[:, span], xt_hbm.at[:, span], xt_sem.at[1])
    last_part.start()
    at = lax.broadcasted_iota(jnp.int32, total_p.shape, 0)
    losses = jnp.sum(jnp.where(at < bits, total_l, 0.0), axis=0, keepdims=True)
    table = jnp.where(at < bits, total_p, jnp.where(at == bits, losses, 0.0))
    filled = jnp.concatenate([table, jnp.zeros((LANES - ROWS, LANES), F32)], axis=0)
    row = lax.dot_general(ones, filled, NT, precision=EXACT, preferred_element_type=F32)
    stat_ref[...] = jnp.broadcast_to(row[:1], stat_ref.shape)
    first_part.wait()
    last_part.wait()


def backward_kernel(
    bits, clip_count, token_count, me_ref,
    h_ref, xt_hbm, base_ref, slope_ref, q_ref, ag_ref, part_ref,
    d_hbm, mine_ref, theirs_ref, loss_ref,
    right_ref, xt_ref, d_ref, xt_sem, d_sem,
):
    frames, tokens, width = h_ref.shape
    arriving = copy(xt_hbm, xt_ref, xt_sem)
    arriving.start()
    leaving = [copy(d_ref.at[f], d_hbm.at[f], d_sem.at[f]) for f in range(frames)]
    core = (me_ref[0] // 2) % 2
    total = jnp.sum(part_ref[...], axis=0, keepdims=True)
    lane = lax.broadcasted_iota(jnp.int32, total.shape, 1)
    mean = jnp.where(lane < bits, total / token_count, 0.5)
    lean = jnp.log((1.0 - mean) / mean)
    entropy = -mean * jnp.log(mean) - (1.0 - mean) * jnp.log(1.0 - mean)
    term = jnp.where(lane < bits, -0.1 * entropy, jnp.where(lane == bits, total / token_count, 0.0))
    loss_ref[...] = jnp.sum(term, axis=1, keepdims=True)
    lean = diagonal(lean, ROWS) * 0.05
    high = ag_ref[:ROWS]
    low = ag_ref[ROWS:]
    right_ref[:, :width] = jnp.concatenate(
        [high, high, low, jnp.zeros((LANES - 3 * ROWS, width), BF16)], axis=0
    )
    at = lax.broadcasted_iota(jnp.int32, (LANES, LANES), 0)
    right_ref[:, width:] = jnp.where((at >= 3 * ROWS) & (at < 5 * ROWS), 1.0, 0.0).astype(BF16)
    step = 256
    for f in range(frames):
        u = (base_ref[f] - slope_ref[f] * lean) * (1.0 / clip_count)
        u_hi, u_lo = hi_lo(u)
        q_hi, q_lo = hi_lo(u * q_ref[f])
        spare = jnp.zeros((LANES - 5 * ROWS, tokens), BF16)
        left = jnp.concatenate([u_hi, u_lo, u_hi, q_hi, q_lo, spare], axis=0).T
        for start in range(0, tokens, step):
            piece = left[start : start + step]
            rows = slice(start, start + step)
            centre = jnp.dot(piece, right_ref[:, width:], preferred_element_type=F32)
            centre = jnp.concatenate([centre, centre], axis=1)
            for col in range(0, width, 2 * LANES):
                cols = slice(col, col + 2 * LANES)
                out = jnp.dot(piece, right_ref[:, cols], preferred_element_type=F32)
                d_ref[f, rows, cols] = (out - centre * h_ref[f, rows, cols].astype(F32)).astype(BF16)
        leaving[f].start()
    block = mine_ref.shape[1]
    group = 8 * block
    arriving.wait()
    for k in range(3):
        count = (frames - k) * tokens
        d_part = d_ref[k:].reshape(count, width)
        for first in range(0, width, GRAD_STEP):
            part = jnp.dot(xt_ref[first : first + GRAD_STEP, :count], d_part, preferred_element_type=F32).astype(BF16)
            base = k * width + first
            for side in range(2):

                @pl.when(core == side)
                def _():
                    row = base
                    while row < base + GRAD_STEP:
                        stop = min((row // block + 1) * block, base + GRAD_STEP)
                        half, within = divmod(row, 2 * group)
                        owner, inside = divmod(within, group)
                        slot, offset = divmod(inside, block)
                        target = mine_ref if owner == side else theirs_ref
                        target[slot * 2 + half, offset : offset + stop - row, :] = part[row - base : stop - base]
                        row = stop
    for one in leaving:
        one.wait()


def input_kernel(
    me_ref, d_hbm, w_hbm, m_hbm, v_hbm,
    out_hbm, mh_ref, vh_ref,
    w_ref, out_ref, d_ref, w_sem, keep_sem, out_sem, d_sem,
):
    frames, tokens, width = d_hbm.shape
    batch, _, sites, _ = out_hbm.shape
    w_copies = [
        copy(w_hbm.at[pl.ds(k * width, width)], w_ref.at[pl.ds(k * width, width)], w_sem.at[k]) for k in range(3)
    ]
    kept = [
        copy(m_hbm, mh_ref, keep_sem.at[0]),
        copy(v_hbm, vh_ref, keep_sem.at[1]),
    ]
    d_copies = [copy(d_hbm.at[f], d_ref.at[f], d_sem.at[f]) for f in range(frames)]
    for i in range(frames):
        d_copies[frames - 1 - i].start()
        if i < 3:
            w_copies[i].start()
    for one in kept:
        one.start()
    sent = []
    for f in range(frames - 1, -1, -1):
        if frames - 1 - f < 3:
            w_copies[frames - 1 - f].wait()
        d_copies[f].wait()
        total = d_ref[f].astype(F32)
        for k in range(min(3, frames - f)):
            total = total + lax.dot_general(
                d_ref[f + k], w_ref[k * width : (k + 1) * width, :], NT, preferred_element_type=F32
            )
        out_ref[f] = total.astype(BF16)
        for c in range(batch):
            one = copy(out_ref.at[f, pl.ds(c * sites, sites)], out_hbm.at[c, f], out_sem.at[f, c])
            one.start()
            sent.append(one)
    for one in kept + sent:
        one.wait()


def updated(weight, first, second, grad):
    first_out = 0.9 * first + 0.1 * grad
    second_out = 0.99 * second + 0.01 * grad * grad
    new = (weight - 0.001 * first_out / (jnp.sqrt(second_out) + 1e-08)).astype(BF16)
    return new, first_out, second_out


def block_kernel(me_ref, parts_ref, w_hbm, mh_ref, vh_ref, send_ref, w_ref, w_sem):
    me = me_ref[0]
    half = me % 2
    core = (me // 2) % 2
    slot = (me // 64) * 2 + (me // 4) % 2
    block = parts_ref.shape[1]
    start = core * 8 * block + slot * block
    rows = pl.ds(pl.multiple_of(start, block), block)
    arriving = copy(w_hbm.at[pl.ds(pl.multiple_of(half * mh_ref.shape[0] + start, block), block)], w_ref, w_sem)
    arriving.start()
    grad = jnp.sum(parts_ref[...].astype(F32), axis=0).astype(BF16)
    arriving.wait()
    new, _, _ = updated(w_ref[...].astype(F32), mh_ref[rows, :], vh_ref[rows, :], grad.astype(F32))
    for d in range(0, send_ref.shape[0], 2):
        send_ref[d + half] = grad
        send_ref[d + 1 - half] = new


def final_kernel(
    side, me_ref, blocks_ref, w_hbm, mh_ref, vh_ref, *refs
):
    new_hbm, first_hbm, second_hbm, new_ref, other_ref, first_ref, second_ref, w_ref, sem, w_sem = refs[-10:]
    half = me_ref[0] % 2
    core = (me_ref[0] // 2) % 2
    owner = core if side == 0 else 1 - core
    slots, block, width = blocks_ref.shape
    owned = mh_ref.shape[0]
    start = pl.multiple_of(owner * (owned // 2), owned // 2)
    rows = 4 * block
    arriving = copy(w_hbm.at[pl.ds(pl.multiple_of(half * owned + start, rows), 2 * rows)], w_ref, w_sem)
    arriving.start()
    arriving.wait()
    sent = []
    for chunk in range(2):
        for j in range(4):
            slot = chunk * 4 + j
            part = pl.ds(pl.multiple_of(start + slot * block, block), block)
            here = pl.ds(slot * block, block)
            grad = blocks_ref[slot * 2 + half].astype(F32)
            new, first_out, second_out = updated(w_ref[here, :].astype(F32), mh_ref[part, :], vh_ref[part, :], grad)
            new_ref[here, :] = new
            other_ref[here, :] = blocks_ref[slot * 2 + 1 - half]
            first_ref[here, :] = first_out
            second_ref[here, :] = second_out
        local = pl.ds(chunk * rows, rows)
        far = pl.ds(pl.multiple_of(start + chunk * rows, rows), rows)
        mine = pl.ds(pl.multiple_of(half * owned + start + chunk * rows, rows), rows)
        peer = pl.ds(pl.multiple_of((1 - half) * owned + start + chunk * rows, rows), rows)
        for i, (source, target, place) in enumerate(
            [(new_ref, new_hbm, mine), (other_ref, new_hbm, peer), (first_ref, first_hbm, far), (second_ref, second_hbm, far)]
        ):
            one = copy(source.at[local], target.at[place], sem.at[chunk, i])
            one.start()
            sent.append(one)
    for one in sent:
        one.wait()


SCALAR = pl.BlockSpec(memory_space=pltpu.SMEM)
NEAR = pl.BlockSpec(memory_space=pltpu.VMEM)
FAR = pl.BlockSpec(memory_space=pltpu.HBM)
DMA = pltpu.SemaphoreType.DMA
PARAMS = pltpu.CompilerParams(vmem_limit_bytes=32 * 1024 * 1024)


def local(value):
    return pltpu.with_memory_space_constraint(value, pltpu.VMEM)


def remote(value):
    return pltpu.with_memory_space_constraint(value, pltpu.HBM)


def run_forward(me, clips, weight, proj, gain, code_bias, rotation, cotangent, devices):
    batch, frames, sites, width = clips.shape
    tokens = batch * sites
    rows = (frames, ROWS, tokens)
    outs = [
        pltpu.VMEM((frames, tokens, width), BF16), pltpu.HBM((width, frames * tokens), BF16),
        pltpu.VMEM(rows, F32), pltpu.VMEM(rows, F32), pltpu.VMEM(rows, F32),
        pltpu.VMEM((2 * ROWS, width), BF16), pltpu.VMEM((devices, LANES), F32),
    ]
    return pl.pallas_call(
        forward_kernel,
        in_specs=[SCALAR] + [FAR] * 7,
        out_specs=[NEAR, FAR] + [NEAR] * 5,
        out_shape=outs,
        scratch_shapes=[
            pltpu.VMEM((frames, tokens, width), BF16), pltpu.VMEM(weight.shape, BF16),
            pltpu.VMEM((ROWS, width), F32), pltpu.VMEM(rows, F32),
            pltpu.VMEM((width, frames * tokens), BF16),
            *[pltpu.VMEM(a.shape, a.dtype) for a in (proj, gain, code_bias, rotation, cotangent)],
            DMA((frames, batch)), DMA((3,)), DMA((2,)), DMA((5,)),
        ],
        compiler_params=PARAMS,
        name="forward",
    )(me, *[remote(a) for a in (clips, weight, proj, gain, code_bias, rotation, cotangent)])


def run_backward(bits, clip_count, token_count, me, saved, ag, parts, row_count):
    width = saved[0].shape[2]
    block = (16, row_count // 32, width)
    return pl.pallas_call(
        functools.partial(backward_kernel, bits, clip_count, token_count),
        in_specs=[SCALAR, NEAR, FAR] + [NEAR] * 5,
        out_specs=[FAR] + [NEAR] * 3,
        out_shape=[
            pltpu.HBM(saved[0].shape, BF16), pltpu.VMEM(block, BF16), pltpu.VMEM(block, BF16),
            jax.ShapeDtypeStruct((1, 1), F32),
        ],
        scratch_shapes=[
            pltpu.VMEM((LANES, width + LANES), BF16), pltpu.VMEM(saved[1].shape, BF16), pltpu.VMEM(saved[0].shape, BF16),
            DMA(()), DMA((saved[0].shape[0],)),
        ],
        compiler_params=PARAMS,
        name="backward",
    )(me, local(saved[0]), remote(saved[1]), *[local(a) for a in (*saved[2:], ag)], local(parts))


def run_input(me, d_conv, weight, first, second, shape):
    batch, frames = shape[:2]
    owned = first.shape
    return pl.pallas_call(
        input_kernel,
        in_specs=[SCALAR] + [FAR] * 4,
        out_specs=[FAR, NEAR, NEAR],
        out_shape=[
            pltpu.HBM(shape, BF16),
            pltpu.VMEM(owned, F32), pltpu.VMEM(owned, F32),
        ],
        scratch_shapes=[
            pltpu.VMEM(weight.shape, BF16), pltpu.VMEM(d_conv.shape, BF16), pltpu.VMEM(d_conv.shape, BF16),
            DMA((3,)), DMA((2,)), DMA((frames, batch)), DMA((frames,)),
        ],
        compiler_params=PARAMS,
        name="input_grad",
    )(me, *[remote(a) for a in (d_conv, weight, first, second)])


def run_block(me, parts, weight, kept):
    send = (16, *parts.shape[1:])
    return pl.pallas_call(
        block_kernel,
        in_specs=[SCALAR, NEAR, FAR, NEAR, NEAR],
        out_specs=NEAR,
        out_shape=pltpu.VMEM(send, BF16),
        scratch_shapes=[pltpu.VMEM(parts.shape[1:], BF16), DMA(())],
        compiler_params=PARAMS,
        name="owner_step",
    )(me, local(parts), remote(weight), *[local(a) for a in kept])


def run_final(side, me, blocks, weight, kept, carried):
    owned, width = kept[0].shape
    shapes = [((2 * owned, width), BF16), ((owned, width), F32), ((owned, width), F32)]
    half = (owned // 2, width)
    return pl.pallas_call(
        functools.partial(final_kernel, side),
        in_specs=[SCALAR, NEAR, FAR, NEAR, NEAR] + [FAR] * len(carried),
        out_specs=[FAR] * 3,
        out_shape=[pltpu.HBM(s, t) for s, t in shapes],
        scratch_shapes=[
            pltpu.VMEM(half, BF16), pltpu.VMEM(half, BF16), pltpu.VMEM(half, F32), pltpu.VMEM(half, F32),
            pltpu.VMEM(half, BF16), DMA((2, 4)), DMA(()),
        ],
        input_output_aliases={5 + i: i for i in range(len(carried))},
        compiler_params=PARAMS,
        name="final_near" if side == 0 else "final_far",
    )(me, local(blocks), remote(weight), *[local(a) for a in kept], *[remote(a) for a in carried])


def spread(value, axes):
    return lax.all_to_all(value, axes, 0, 0, tiled=True)


def swapped(value):
    return lax.ppermute(value, "core", [(0, 1), (1, 0)])


def on_device(clips, code_grad, conv_weight, norm_gain, proj_weight, code_bias, rotation, first_moment, second_moment):
    bits = code_grad.shape[3]
    devices = lax.axis_size(ALL)
    batch, frames, sites, width = clips.shape
    clip_count = batch * devices
    token_count = clip_count * frames * sites
    me = lax.axis_index(ALL).astype(jnp.int32).reshape(1)
    cotangent = code_grad.transpose(1, 3, 0, 2)
    *saved, ag, stats = run_forward(
        me, clips, conv_weight, proj_weight.T, norm_gain[None, :], code_bias[None, :], rotation, cotangent, devices
    )
    parts = spread(stats, ALL)
    d_conv, mine, theirs, loss = run_backward(
        bits, clip_count, token_count, me, saved, ag, parts, conv_weight.shape[0]
    )
    chip = (mine.astype(F32) + swapped(theirs).astype(F32)).astype(BF16)
    plane = spread(chip, PLANE)
    input_grad, *kept = run_input(me, d_conv, conv_weight, first_moment, second_moment, clips.shape)
    plane, kept = lax.optimization_barrier((plane, kept))
    column = jnp.sum(plane.astype(F32), axis=0).astype(BF16)
    tower = spread(jnp.broadcast_to(column, (lax.axis_size("z"), *column.shape)), "z")
    near = spread(run_block(me, tower, conv_weight, kept), PLANE)
    far = swapped(near)
    carried = run_final(0, me, near, conv_weight, kept, [])
    new_weight, first_out, second_out = run_final(1, me, far, conv_weight, kept, carried)
    return new_weight, first_out, second_out, input_grad, loss[0, 0]


def solution(mesh):
    finer = Mesh(mesh.devices.reshape(4, 8, 2, 2, mesh.shape["shard"]), ALL)
    split = P(ALL, None, None, None)
    in_specs = (split, split, P(), P(), P(), P(), P(), P("yl", None), P("yl", None))
    out_specs = (P(), P("yl", None), P("yl", None), split, P())
    return jax.shard_map(on_device, mesh=finer, in_specs=in_specs, out_specs=out_specs, check_vma=False)
```

```python
import functools

import jax
import jax.numpy as jnp
from jax import lax
from jax.experimental import pallas as pl
from jax.experimental.pallas import tpu as pltpu
from jax.sharding import Mesh
from jax.sharding import PartitionSpec as P

ALL = ("x", "z", "yh", "core", "yl")
CHIPS = ("x", "z", "yh", "yl")
PLANE = ("x", "yh", "yl")
ROWS = 24
ROW_STEP = 512
COL_STEP = 512
GRAD_STEP = 512
LANES = 128
F32 = jnp.float32
BF16 = jnp.bfloat16
NT = (((1,), (1,)), ((), ()))
TN = (((0,), (0,)), ((), ()))
EXACT = lax.Precision.HIGHEST


def hi_lo(value):
    high = value.astype(BF16)
    return high, (value - high.astype(F32)).astype(BF16)


def diagonal(row, count):
    grid = jnp.broadcast_to(row, (count, row.shape[1]))
    at = lax.broadcasted_iota(jnp.int32, grid.shape, 0)
    to = lax.broadcasted_iota(jnp.int32, grid.shape, 1)
    return jnp.sum(jnp.where(at == to, grid, 0.0), axis=1, keepdims=True)


def lane_groups(value):
    part = value[:, :LANES]
    for g in range(1, value.shape[1] // LANES):
        part = part + value[:, g * LANES : (g + 1) * LANES]
    return part


def copy(source, target, sem):
    return pltpu.make_async_copy(source, target, sem)


def forward_kernel(
    _, x_hbm, w_hbm, proj_hbm, gain_hbm, code_bias_hbm, rotation_hbm, cg_hbm,
    h_ref, raw_ref, inv_ref, bias_ref, cot_ref, ag_ref, stat_ref,
    x_ref, w_ref, map_ref, proj_ref, gain_ref, code_bias_ref, rotation_ref, cg_ref,
    x_sem, w_sem, small_sem,
):
    batch, frames, sites, width = x_hbm.shape
    bits = rotation_ref.shape[0]
    tokens = batch * sites
    pairs = [
        (proj_hbm, proj_ref), (gain_hbm, gain_ref), (code_bias_hbm, code_bias_ref),
        (rotation_hbm, rotation_ref), (cg_hbm, cg_ref),
    ]
    small_copies = [copy(a, b, small_sem.at[i]) for i, (a, b) in enumerate(pairs)]
    for one in small_copies:
        one.start()
    x_copies = [
        [copy(x_hbm.at[c, f], x_ref.at[f, pl.ds(c * sites, sites)], x_sem.at[f, c]) for c in range(batch)]
        for f in range(frames)
    ]
    w_copies = [
        copy(w_hbm.at[pl.ds(k * width, width)], w_ref.at[pl.ds(k * width, width)], w_sem.at[k]) for k in range(3)
    ]
    for f in range(frames):
        for one in x_copies[f]:
            one.start()
        if f < 3:
            w_copies[f].start()
    map_ref[...] = jnp.zeros_like(map_ref)
    cot_ref[...] = jnp.zeros_like(cot_ref)
    for one in small_copies:
        one.wait()
    map_ref[:bits, :] = (
        lax.dot_general(
            rotation_ref[...], proj_ref[...].astype(F32), TN, precision=EXACT, preferred_element_type=F32
        )
        * gain_ref[...]
    )
    row = jnp.dot(code_bias_ref[...], rotation_ref[...], precision=EXACT, preferred_element_type=F32)
    bias = diagonal(jnp.concatenate([row, jnp.zeros((1, LANES - bits), F32)], axis=1), ROWS)
    bias_ref[...] = jnp.broadcast_to(bias, bias_ref.shape)
    high, low = hi_lo(map_ref[...])
    ag_ref[...] = jnp.concatenate([high, low], axis=0)
    ones = jnp.ones((8, LANES), F32)
    total_p = jnp.zeros((ROWS, LANES), F32)
    total_l = jnp.zeros((ROWS, LANES), F32)
    def multiply(f):
        means = []
        for start in range(0, tokens, ROW_STEP):
            rows = slice(start, start + ROW_STEP)
            part = jnp.zeros((ROW_STEP, LANES), F32)
            for first in range(0, width, COL_STEP):
                cols = slice(first, first + COL_STEP)
                hidden = x_ref[f, rows, cols].astype(F32)
                for k in range(min(f, 2) + 1):
                    hidden = hidden + jnp.dot(
                        x_ref[f - k, rows, :], w_ref[k * width : (k + 1) * width, cols], preferred_element_type=F32
                    )
                h_ref[f, rows, cols] = hidden.astype(BF16)
                part = part + lane_groups(hidden * hidden)
            means.append(lax.dot_general(ones, part, NT, preferred_element_type=F32)[:1] / width)
        both = lax.dot_general(ag_ref[...], h_ref[f], NT, preferred_element_type=F32)
        return jnp.concatenate(means, axis=1), both[:ROWS] + both[ROWS:]

    def decide(f, mean, raw):
        inv = lax.rsqrt(mean + 1e-06)
        rotated = raw * inv + bias
        cot_ref[f, :bits, :sites] = cg_ref[f, :, 0, :].astype(F32)
        cot_ref[f, :bits, sites:] = cg_ref[f, :, 1, :].astype(F32)
        cotangent = cot_ref[f]
        small = jnp.exp(-2.0 * jnp.abs(rotated))
        size = (1.0 - small) / (1.0 + small)
        codes = jnp.where(rotated < 0.0, -size, size)
        probs = 0.5 + 0.5 * codes
        logit = 2.0 * rotated
        gap = rotated - codes
        entropy = jnp.maximum(logit, 0.0) + jnp.log(1.0 + small) - logit * probs
        raw_ref[f] = raw
        inv_ref[f] = jnp.broadcast_to(inv, inv_ref.shape[1:])
        return lane_groups(probs), lane_groups(cotangent * codes + 0.25 * gap * gap + 0.1 * entropy)

    def arrive(f):
        for one in x_copies[f]:
            one.wait()
        if f < 3:
            w_copies[f].wait()

    waiting = []
    for f in range(frames):
        arrive(f)
        ready = multiply(f)
        for earlier in waiting:
            sums = decide(*earlier)
            total_p = total_p + sums[0]
            total_l = total_l + sums[1]
        waiting = [(f, *ready)]
    sums = decide(*waiting[0])
    total_p = total_p + sums[0]
    total_l = total_l + sums[1]
    at = lax.broadcasted_iota(jnp.int32, total_p.shape, 0)
    losses = jnp.sum(jnp.where(at < bits, total_l, 0.0), axis=0, keepdims=True)
    table = jnp.where(at < bits, total_p, jnp.where(at == bits, losses, 0.0))
    filled = jnp.concatenate([table, jnp.zeros((LANES - ROWS, LANES), F32)], axis=0)
    row = lax.dot_general(ones, filled, NT, precision=EXACT, preferred_element_type=F32)
    stat_ref[...] = jnp.broadcast_to(row[:1], stat_ref.shape)


def window_kernel(
    x_hbm, h_ref, raw_ref, inv_ref, bias_ref, cot_ref,
    h_hbm, xt_hbm, rows_hbm,
    x_ref, xt_ref, rows_ref, x_sem, xt_sem, h_sem, rows_sem,
):
    batch, frames, sites, width = x_hbm.shape
    tokens = batch * sites
    arriving = [
        copy(x_hbm.at[c, f], x_ref.at[f, pl.ds(c * sites, sites)], x_sem.at[f, c])
        for f in range(frames)
        for c in range(batch)
    ]
    for one in arriving:
        one.start()
    moved = copy(h_ref, h_hbm, h_sem)
    moved.start()
    bias = bias_ref[:, :1]
    for f in range(frames):
        raw = raw_ref[f]
        inv = inv_ref[f][:1]
        rotated = raw * inv + bias
        cotangent = cot_ref[f]
        small = jnp.exp(-2.0 * jnp.abs(rotated))
        size = (1.0 - small) / (1.0 + small)
        codes = jnp.where(rotated < 0.0, -size, size)
        slope = 1.0 - codes * codes
        base = cotangent * slope + 0.5 * (rotated - codes) * (1.0 - slope) - 0.1 * rotated * slope
        rows_ref[f, 0] = base * inv
        rows_ref[f, 1] = slope * inv
        rows_ref[f, 2] = raw * (inv * inv) / width
    gone = copy(rows_ref, rows_hbm, rows_sem)
    gone.start()
    for one in arriving:
        one.wait()
    for f in range(frames):
        xt_ref[:, f * tokens : (f + 1) * tokens] = x_ref[f].T
    leaving = copy(xt_ref, xt_hbm, xt_sem)
    leaving.start()
    leaving.wait()
    moved.wait()
    gone.wait()


def backward_kernel(
    bits, clip_count, token_count, me_ref,
    h_hbm, xt_hbm, rows_hbm, ag_ref, part_ref,
    d_hbm, both_ref, loss_ref,
    right_ref, xt_ref, d_ref, grad_ref, h_ref, rows_ref, xt_sem, d_sem, h_sem, rows_sem,
):
    frames, tokens, width = h_hbm.shape
    h_copies = [copy(h_hbm.at[f], h_ref.at[f], h_sem.at[f]) for f in range(frames)]
    rows_copies = [copy(rows_hbm.at[f], rows_ref.at[f], rows_sem.at[f]) for f in range(frames)]
    for f in range(frames):
        rows_copies[f].start()
        h_copies[f].start()
    arriving = copy(xt_hbm, xt_ref, xt_sem)
    arriving.start()
    leaving = [copy(d_ref.at[f], d_hbm.at[f], d_sem.at[f]) for f in range(frames)]
    core = (me_ref[0] // 2) % 2
    total = jnp.sum(part_ref[...], axis=0, keepdims=True)
    lane = lax.broadcasted_iota(jnp.int32, total.shape, 1)
    mean = jnp.where(lane < bits, total / token_count, 0.5)
    lean = jnp.log((1.0 - mean) / mean)
    entropy = -mean * jnp.log(mean) - (1.0 - mean) * jnp.log(1.0 - mean)
    term = jnp.where(lane < bits, -0.1 * entropy, jnp.where(lane == bits, total / token_count, 0.0))
    loss_ref[...] = jnp.sum(term, axis=1, keepdims=True)
    lean = diagonal(lean, ROWS) * 0.05
    high = ag_ref[:ROWS]
    low = ag_ref[ROWS:]
    right_ref[...] = jnp.concatenate(
        [high, high, low, jnp.zeros((LANES - 3 * ROWS, width), BF16)], axis=0
    )
    step = 256
    for f in range(frames):
        for other in {0: [0], 1: range(1, frames)}.get(f, []):
            rows_copies[other].wait()
            h_copies[other].wait()
        u = (rows_ref[f, 0] - rows_ref[f, 1] * lean) * (1.0 / clip_count)
        u_hi, u_lo = hi_lo(u)
        centres = jnp.sum(u * rows_ref[f, 2], axis=0, keepdims=True)
        centres = jnp.broadcast_to(centres, (8, tokens)).T
        spare = jnp.zeros((LANES - 3 * ROWS, tokens), BF16)
        left = jnp.concatenate([u_hi, u_lo, u_hi, spare], axis=0).T
        for start in range(0, tokens, step):
            piece = left[start : start + step]
            rows = slice(start, start + step)
            centre = jnp.broadcast_to(centres[rows, :1], (step, 2 * LANES))
            for col in range(0, width, 2 * LANES):
                cols = slice(col, col + 2 * LANES)
                out = jnp.dot(piece, right_ref[:, cols], preferred_element_type=F32)
                d_ref[f, rows, cols] = (out - centre * h_ref[f, rows, cols].astype(F32)).astype(BF16)
        leaving[f].start()
    block = both_ref.shape[2]
    group = 8 * block
    arriving.wait()
    for k in range(3):
        count = (frames - k) * tokens
        d_part = d_ref[k:].reshape(count, width)
        base = k * width
        grad_ref[base : base + width, :] = jnp.dot(xt_ref[:, :count], d_part, preferred_element_type=F32).astype(BF16)
    for k in range(3):
        base = k * width
        row = base
        while row < base + width:
            stop = min((row // block + 1) * block, base + width)
            half, within = divmod(row, 2 * group)
            owner, inside = divmod(within, group)
            slot, offset = divmod(inside, block)
            where = core if owner == 0 else 1 - core
            both_ref[where, slot * 2 + half, offset : offset + stop - row, :] = grad_ref[row:stop, :]
            row = stop
    for one in leaving:
        one.wait()


def input_kernel(
    me_ref, d_hbm, w_hbm, m_hbm, v_hbm,
    out_hbm, mh_ref, vh_ref,
    w_ref, out_ref, d_ref, w_sem, keep_sem, out_sem, d_sem,
):
    frames, tokens, width = d_hbm.shape
    batch, _, sites, _ = out_hbm.shape
    w_copies = [
        copy(w_hbm.at[pl.ds(k * width, width)], w_ref.at[pl.ds(k * width, width)], w_sem.at[k]) for k in range(3)
    ]
    kept = [
        copy(m_hbm, mh_ref, keep_sem.at[0]),
        copy(v_hbm, vh_ref, keep_sem.at[1]),
    ]
    d_copies = [copy(d_hbm.at[f], d_ref.at[f], d_sem.at[f]) for f in range(frames)]
    for i in range(frames):
        d_copies[frames - 1 - i].start()
        if i < 3:
            w_copies[i].start()
    for one in kept:
        one.start()
    sent = []
    for f in range(frames - 1, -1, -1):
        if frames - 1 - f < 3:
            w_copies[frames - 1 - f].wait()
        d_copies[f].wait()
        total = d_ref[f].astype(F32)
        for k in range(min(3, frames - f)):
            total = total + lax.dot_general(
                d_ref[f + k], w_ref[k * width : (k + 1) * width, :], NT, preferred_element_type=F32
            )
        out_ref[f] = total.astype(BF16)
        for c in range(batch):
            one = copy(out_ref.at[f, pl.ds(c * sites, sites)], out_hbm.at[c, f], out_sem.at[f, c])
            one.start()
            sent.append(one)
    for one in kept + sent:
        one.wait()


def updated(weight, first, second, grad):
    first_out = 0.9 * first + 0.1 * grad
    second_out = 0.99 * second + 0.01 * grad * grad
    new = (weight - 0.001 * first_out / (jnp.sqrt(second_out) + 1e-08)).astype(BF16)
    return new, first_out, second_out


def block_kernel(me_ref, parts_ref, w_hbm, mh_ref, vh_ref, send_ref, w_ref, w_sem):
    me = me_ref[0]
    half = me % 2
    core = (me // 2) % 2
    slot = (me // 64) * 2 + (me // 4) % 2
    block = parts_ref.shape[1]
    start = core * 8 * block + slot * block
    rows = pl.ds(pl.multiple_of(start, block), block)
    arriving = copy(w_hbm.at[pl.ds(pl.multiple_of(half * mh_ref.shape[0] + start, block), block)], w_ref, w_sem)
    arriving.start()
    grad = jnp.sum(parts_ref[...].astype(F32), axis=0).astype(BF16)
    arriving.wait()
    new, _, _ = updated(w_ref[...].astype(F32), mh_ref[rows, :], vh_ref[rows, :], grad.astype(F32))
    for d in range(0, send_ref.shape[0], 2):
        send_ref[d + half] = grad
        send_ref[d + 1 - half] = new


def final_kernel(side, me_ref, blocks_ref, *refs):
    half = me_ref[0] % 2
    core = (me_ref[0] // 2) % 2
    owner = core if side == 0 else 1 - core
    slots, block, width = blocks_ref.shape
    if side == 0:
        w_hbm, mh_ref, vh_ref = refs[:3]
        new_hbm, first_hbm, second_hbm, w_next, new_ref, first_ref, second_ref, w_ref, sem, other_sem, w_sem = refs[3:]
    else:
        w_ref, mh_ref, vh_ref = refs[:3]
        new_hbm, first_hbm, second_hbm, new_ref, first_ref, second_ref, sem, other_sem = refs[6:]
    owned = mh_ref.shape[0]
    side_rows = owned // 2
    start = pl.multiple_of(owner * side_rows, side_rows)
    if side == 0:
        next_start = pl.multiple_of(half * owned + (1 - owner) * side_rows, side_rows)
        near_w = copy(w_hbm.at[pl.ds(pl.multiple_of(half * owned + start, side_rows), side_rows)], w_ref, w_sem.at[0])
        far_w = copy(w_hbm.at[pl.ds(next_start, side_rows)], w_next, w_sem.at[1])
        near_w.start()
        far_w.start()
    sent = []
    for slot in range(slots // 2):
        peer = pl.multiple_of((1 - half) * owned + start + slot * block, block)
        sent.append(copy(blocks_ref.at[slot * 2 + 1 - half], new_hbm.at[pl.ds(peer, block)], other_sem.at[slot]))
        sent[-1].start()
    if side == 0:
        near_w.wait()
    per = 2
    rows = per * block
    for chunk in range(slots // 2 // per):
        for j in range(per):
            slot = chunk * per + j
            part = pl.ds(pl.multiple_of(start + slot * block, block), block)
            here = pl.ds(slot * block, block)
            grad = blocks_ref[slot * 2 + half].astype(F32)
            new, first_out, second_out = updated(w_ref[here, :].astype(F32), mh_ref[part, :], vh_ref[part, :], grad)
            new_ref[here, :] = new
            first_ref[here, :] = first_out
            second_ref[here, :] = second_out
        local = pl.ds(chunk * rows, rows)
        far = pl.ds(pl.multiple_of(start + chunk * rows, rows), rows)
        mine = pl.ds(pl.multiple_of(half * owned + start + chunk * rows, rows), rows)
        for i, (source, target, place) in enumerate(
            [(new_ref, new_hbm, mine), (first_ref, first_hbm, far), (second_ref, second_hbm, far)]
        ):
            one = copy(source.at[local], target.at[place], sem.at[chunk, i])
            one.start()
            sent.append(one)
    for one in sent:
        one.wait()
    if side == 0:
        far_w.wait()


SCALAR = pl.BlockSpec(memory_space=pltpu.SMEM)
NEAR = pl.BlockSpec(memory_space=pltpu.VMEM)
FAR = pl.BlockSpec(memory_space=pltpu.HBM)
DMA = pltpu.SemaphoreType.DMA
PARAMS = pltpu.CompilerParams(vmem_limit_bytes=32 * 1024 * 1024)


def local(value):
    return pltpu.with_memory_space_constraint(value, pltpu.VMEM)


def remote(value):
    return pltpu.with_memory_space_constraint(value, pltpu.HBM)


def run_forward(me, clips, weight, proj, gain, code_bias, rotation, cotangent, devices):
    batch, frames, sites, width = clips.shape
    tokens = batch * sites
    rows = (frames, ROWS, tokens)
    outs = [
        pltpu.VMEM((frames, tokens, width), BF16), pltpu.VMEM(rows, F32), pltpu.VMEM((frames, 8, tokens), F32),
        pltpu.VMEM((ROWS, LANES), F32), pltpu.VMEM(rows, F32),
        pltpu.VMEM((2 * ROWS, width), BF16), pltpu.VMEM((devices, LANES), F32),
    ]
    return pl.pallas_call(
        forward_kernel,
        in_specs=[SCALAR] + [FAR] * 7,
        out_specs=[NEAR] * 7,
        out_shape=outs,
        scratch_shapes=[
            pltpu.VMEM((frames, tokens, width), BF16), pltpu.VMEM(weight.shape, BF16),
            pltpu.VMEM((ROWS, width), F32),
            *[pltpu.VMEM(a.shape, a.dtype) for a in (proj, gain, code_bias, rotation, cotangent)],
            DMA((frames, batch)), DMA((3,)), DMA((5,)),
        ],
        compiler_params=PARAMS,
        name="forward",
    )(me, *[remote(a) for a in (clips, weight, proj, gain, code_bias, rotation, cotangent)])


def run_window(clips, hidden, raw, inv, bias, cot):
    batch, frames, sites, width = clips.shape
    tokens = batch * sites
    return pl.pallas_call(
        window_kernel,
        in_specs=[FAR] + [NEAR] * 5,
        out_specs=[FAR] * 3,
        out_shape=[
            pltpu.HBM(hidden.shape, BF16), pltpu.HBM((width, frames * tokens), BF16),
            pltpu.HBM((frames, 3, *raw.shape[1:]), F32),
        ],
        scratch_shapes=[
            pltpu.VMEM((frames, tokens, width), BF16), pltpu.VMEM((width, frames * tokens), BF16),
            pltpu.VMEM((frames, 3, *raw.shape[1:]), F32), DMA((frames, batch)), DMA(()), DMA(()), DMA(()),
        ],
        compiler_params=PARAMS,
        name="window",
    )(remote(clips), *[local(a) for a in (hidden, raw, inv, bias, cot)])


def run_backward(bits, clip_count, token_count, me, saved, ag, parts, row_count):
    width = saved[0].shape[2]
    both = (2, 16, row_count // 32, width)
    return pl.pallas_call(
        functools.partial(backward_kernel, bits, clip_count, token_count),
        in_specs=[SCALAR] + [FAR] * 3 + [NEAR] * 2,
        out_specs=[FAR] + [NEAR] * 2,
        out_shape=[
            pltpu.HBM(saved[0].shape, BF16), pltpu.VMEM(both, BF16),
            jax.ShapeDtypeStruct((1, 1), F32),
        ],
        scratch_shapes=[
            pltpu.VMEM((LANES, width), BF16), pltpu.VMEM(saved[1].shape, BF16), pltpu.VMEM(saved[0].shape, BF16),
            pltpu.VMEM((row_count, width), BF16), pltpu.VMEM(saved[0].shape, BF16),
            pltpu.VMEM(saved[2].shape, F32),
            DMA(()), *[DMA((saved[0].shape[0],))] * 3,
        ],
        compiler_params=PARAMS,
        name="backward",
    )(me, *[remote(a) for a in saved], local(ag), local(parts))


def run_input(me, d_conv, weight, first, second, shape):
    batch, frames = shape[:2]
    owned = first.shape
    return pl.pallas_call(
        input_kernel,
        in_specs=[SCALAR] + [FAR] * 4,
        out_specs=[FAR, NEAR, NEAR],
        out_shape=[
            pltpu.HBM(shape, BF16),
            pltpu.VMEM(owned, F32), pltpu.VMEM(owned, F32),
        ],
        scratch_shapes=[
            pltpu.VMEM(weight.shape, BF16), pltpu.VMEM(d_conv.shape, BF16), pltpu.VMEM(d_conv.shape, BF16),
            DMA((3,)), DMA((2,)), DMA((frames, batch)), DMA((frames,)),
        ],
        compiler_params=PARAMS,
        name="input_grad",
    )(me, *[remote(a) for a in (d_conv, weight, first, second)])


def run_block(me, parts, weight, kept):
    send = (16, *parts.shape[1:])
    return pl.pallas_call(
        block_kernel,
        in_specs=[SCALAR, NEAR, FAR, NEAR, NEAR],
        out_specs=NEAR,
        out_shape=pltpu.VMEM(send, BF16),
        scratch_shapes=[pltpu.VMEM(parts.shape[1:], BF16), DMA(())],
        compiler_params=PARAMS,
        name="owner_step",
    )(me, local(parts), remote(weight), *[local(a) for a in kept])


def run_final(side, me, blocks, weight, kept, carried):
    owned, width = kept[0].shape
    shapes = [((2 * owned, width), BF16), ((owned, width), F32), ((owned, width), F32)]
    half = (owned // 2, width)
    outs = [pltpu.HBM(s, t) for s, t in shapes]
    scratch = [pltpu.VMEM(half, BF16), pltpu.VMEM(half, F32), pltpu.VMEM(half, F32)]
    sems = [DMA((4, 3)), DMA((8,))]
    if side == 0:
        outs.append(pltpu.VMEM(half, BF16))
        scratch.append(pltpu.VMEM(half, BF16))
        sems.append(DMA((2,)))
    return pl.pallas_call(
        functools.partial(final_kernel, side),
        in_specs=[SCALAR, NEAR, FAR if side == 0 else NEAR, NEAR, NEAR] + [FAR] * len(carried),
        out_specs=[FAR] * 3 + [NEAR] * (1 - side),
        out_shape=outs,
        scratch_shapes=scratch + sems,
        input_output_aliases={5 + i: i for i in range(len(carried))},
        compiler_params=PARAMS,
        name="final_near" if side == 0 else "final_far",
    )(
        me, local(blocks), (remote if side == 0 else local)(weight),
        *[local(a) for a in kept], *[remote(a) for a in carried],
    )


def spread(value, axes):
    return lax.all_to_all(value, axes, 0, 0, tiled=True)


def swapped(value):
    return lax.ppermute(value, "core", [(0, 1), (1, 0)])


def on_device(clips, code_grad, conv_weight, norm_gain, proj_weight, code_bias, rotation, first_moment, second_moment):
    bits = code_grad.shape[3]
    devices = lax.axis_size(ALL)
    batch, frames, sites, width = clips.shape
    clip_count = batch * devices
    token_count = clip_count * frames * sites
    me = lax.axis_index(ALL).astype(jnp.int32).reshape(1)
    cotangent = code_grad.transpose(1, 3, 0, 2)
    hidden, raw, inv, bias, cot, ag, stats = run_forward(
        me, clips, conv_weight, proj_weight.T, norm_gain[None, :], code_bias[None, :], rotation, cotangent, lax.axis_size(CHIPS)
    )
    parts = spread(stats + swapped(stats), CHIPS)
    saved = run_window(clips, hidden, raw, inv, bias, cot)
    d_conv, both, loss = run_backward(
        bits, clip_count, token_count, me, saved, ag, parts, conv_weight.shape[0]
    )
    chip = (both[0].astype(F32) + swapped(both[1]).astype(F32)).astype(BF16)
    plane = spread(chip, PLANE)
    input_grad, *kept = run_input(me, d_conv, conv_weight, first_moment, second_moment, clips.shape)
    plane, kept = lax.optimization_barrier((plane, kept))
    column = jnp.sum(plane.astype(F32), axis=0).astype(BF16)
    tower = spread(jnp.broadcast_to(column, (lax.axis_size("z"), *column.shape)), "z")
    near = spread(run_block(me, tower, conv_weight, kept), PLANE)
    far = swapped(near)
    *carried, w_far = run_final(0, me, near, conv_weight, kept, [])
    new_weight, first_out, second_out = run_final(1, me, far, w_far, kept, carried)
    return new_weight, first_out, second_out, input_grad, loss[0, 0]


def solution(mesh):
    finer = Mesh(mesh.devices.reshape(4, 8, 2, 2, mesh.shape["shard"]), ALL)
    split = P(ALL, None, None, None)
    in_specs = (split, split, P(), P(), P(), P(), P(), P("yl", None), P("yl", None))
    out_specs = (P(), P("yl", None), P("yl", None), split, P())
    return jax.shard_map(on_device, mesh=finer, in_specs=in_specs, out_specs=out_specs, check_vma=False)
```

```python
import functools

import jax
import jax.numpy as jnp
from jax import lax
from jax.experimental import pallas as pl
from jax.experimental.pallas import tpu as pltpu
from jax.sharding import Mesh
from jax.sharding import PartitionSpec as P

ALL = ("x", "z", "yh", "core", "yl")
PLANE = ("x", "yh", "yl")
ROWS = 24
ROW_STEP = 512
COL_STEP = 512
GRAD_STEP = 512
LANES = 128
F32 = jnp.float32
BF16 = jnp.bfloat16
NT = (((1,), (1,)), ((), ()))
TN = (((0,), (0,)), ((), ()))
EXACT = lax.Precision.HIGHEST


def hi_lo(value):
    high = value.astype(BF16)
    return high, (value - high.astype(F32)).astype(BF16)


def diagonal(row, count):
    grid = jnp.broadcast_to(row, (count, row.shape[1]))
    at = lax.broadcasted_iota(jnp.int32, grid.shape, 0)
    to = lax.broadcasted_iota(jnp.int32, grid.shape, 1)
    return jnp.sum(jnp.where(at == to, grid, 0.0), axis=1, keepdims=True)


def lane_groups(value):
    part = value[:, :LANES]
    for g in range(1, value.shape[1] // LANES):
        part = part + value[:, g * LANES : (g + 1) * LANES]
    return part


def copy(source, target, sem):
    return pltpu.make_async_copy(source, target, sem)


def forward_kernel(
    _, x_hbm, w_hbm, proj_hbm, gain_hbm, code_bias_hbm, rotation_hbm, cg_hbm,
    h_ref, raw_ref, inv_ref, bias_ref, cot_ref, ag_ref, stat_ref,
    x_ref, w_ref, map_ref, proj_ref, gain_ref, code_bias_ref, rotation_ref, cg_ref,
    x_sem, w_sem, small_sem,
):
    batch, frames, sites, width = x_hbm.shape
    bits = rotation_ref.shape[0]
    tokens = batch * sites
    pairs = [
        (proj_hbm, proj_ref), (gain_hbm, gain_ref), (code_bias_hbm, code_bias_ref),
        (rotation_hbm, rotation_ref), (cg_hbm, cg_ref),
    ]
    small_copies = [copy(a, b, small_sem.at[i]) for i, (a, b) in enumerate(pairs)]
    for one in small_copies:
        one.start()
    x_copies = [
        [copy(x_hbm.at[c, f], x_ref.at[f, pl.ds(c * sites, sites)], x_sem.at[f, c]) for c in range(batch)]
        for f in range(frames)
    ]
    w_copies = [
        copy(w_hbm.at[pl.ds(k * width, width)], w_ref.at[pl.ds(k * width, width)], w_sem.at[k]) for k in range(3)
    ]
    for f in range(frames):
        for one in x_copies[f]:
            one.start()
        if f < 3:
            w_copies[f].start()
    map_ref[...] = jnp.zeros_like(map_ref)
    cot_ref[...] = jnp.zeros_like(cot_ref)
    for one in small_copies:
        one.wait()
    map_ref[:bits, :] = (
        lax.dot_general(
            rotation_ref[...], proj_ref[...].astype(F32), TN, precision=EXACT, preferred_element_type=F32
        )
        * gain_ref[...]
    )
    row = jnp.dot(code_bias_ref[...], rotation_ref[...], precision=EXACT, preferred_element_type=F32)
    bias = diagonal(jnp.concatenate([row, jnp.zeros((1, LANES - bits), F32)], axis=1), ROWS)
    bias_ref[...] = jnp.broadcast_to(bias, bias_ref.shape)
    high, low = hi_lo(map_ref[...])
    ag_ref[...] = jnp.concatenate([high, low], axis=0)
    ones = jnp.ones((8, LANES), F32)
    total_p = jnp.zeros((ROWS, LANES), F32)
    total_l = jnp.zeros((ROWS, LANES), F32)
    def multiply(f):
        means = []
        for start in range(0, tokens, ROW_STEP):
            rows = slice(start, start + ROW_STEP)
            part = jnp.zeros((ROW_STEP, LANES), F32)
            for first in range(0, width, COL_STEP):
                cols = slice(first, first + COL_STEP)
                hidden = x_ref[f, rows, cols].astype(F32)
                for k in range(min(f, 2) + 1):
                    hidden = hidden + jnp.dot(
                        x_ref[f - k, rows, :], w_ref[k * width : (k + 1) * width, cols], preferred_element_type=F32
                    )
                h_ref[f, rows, cols] = hidden.astype(BF16)
                part = part + lane_groups(hidden * hidden)
            means.append(lax.dot_general(ones, part, NT, preferred_element_type=F32)[:1] / width)
        both = lax.dot_general(ag_ref[...], h_ref[f], NT, preferred_element_type=F32)
        return jnp.concatenate(means, axis=1), both[:ROWS] + both[ROWS:]

    def decide(f, mean, raw):
        inv = lax.rsqrt(mean + 1e-06)
        rotated = raw * inv + bias
        cot_ref[f, :bits, :sites] = cg_ref[f, :, 0, :].astype(F32)
        cot_ref[f, :bits, sites:] = cg_ref[f, :, 1, :].astype(F32)
        cotangent = cot_ref[f]
        small = jnp.exp(-2.0 * jnp.abs(rotated))
        size = (1.0 - small) / (1.0 + small)
        codes = jnp.where(rotated < 0.0, -size, size)
        probs = 0.5 + 0.5 * codes
        logit = 2.0 * rotated
        gap = rotated - codes
        entropy = jnp.maximum(logit, 0.0) + jnp.log(1.0 + small) - logit * probs
        raw_ref[f] = raw
        inv_ref[f] = jnp.broadcast_to(inv, inv_ref.shape[1:])
        return lane_groups(probs), lane_groups(cotangent * codes + 0.25 * gap * gap + 0.1 * entropy)

    def arrive(f):
        for one in x_copies[f]:
            one.wait()
        if f < 3:
            w_copies[f].wait()

    waiting = []
    for f in range(frames):
        arrive(f)
        ready = multiply(f)
        for earlier in waiting:
            sums = decide(*earlier)
            total_p = total_p + sums[0]
            total_l = total_l + sums[1]
        waiting = [(f, *ready)]
    sums = decide(*waiting[0])
    total_p = total_p + sums[0]
    total_l = total_l + sums[1]
    at = lax.broadcasted_iota(jnp.int32, total_p.shape, 0)
    losses = jnp.sum(jnp.where(at < bits, total_l, 0.0), axis=0, keepdims=True)
    table = jnp.where(at < bits, total_p, jnp.where(at == bits, losses, 0.0))
    filled = jnp.concatenate([table, jnp.zeros((LANES - ROWS, LANES), F32)], axis=0)
    row = lax.dot_general(ones, filled, NT, precision=EXACT, preferred_element_type=F32)
    stat_ref[...] = jnp.broadcast_to(row[:1], stat_ref.shape)


def window_kernel(
    x_hbm, h_ref, raw_ref, inv_ref, bias_ref, cot_ref,
    h_hbm, xt_hbm, rows_hbm,
    x_ref, xt_ref, rows_ref, x_sem, xt_sem, h_sem, rows_sem,
):
    batch, frames, sites, width = x_hbm.shape
    tokens = batch * sites
    arriving = [
        copy(x_hbm.at[c, f], x_ref.at[f, pl.ds(c * sites, sites)], x_sem.at[f, c])
        for f in range(frames)
        for c in range(batch)
    ]
    for one in arriving:
        one.start()
    moved = copy(h_ref, h_hbm, h_sem)
    moved.start()
    bias = bias_ref[:, :1]
    for f in range(frames):
        raw = raw_ref[f]
        inv = inv_ref[f][:1]
        rotated = raw * inv + bias
        cotangent = cot_ref[f]
        small = jnp.exp(-2.0 * jnp.abs(rotated))
        size = (1.0 - small) / (1.0 + small)
        codes = jnp.where(rotated < 0.0, -size, size)
        slope = 1.0 - codes * codes
        base = cotangent * slope + 0.5 * (rotated - codes) * (1.0 - slope) - 0.1 * rotated * slope
        rows_ref[f, 0] = base * inv
        rows_ref[f, 1] = slope * inv
        rows_ref[f, 2] = raw * (inv * inv) / width
    gone = copy(rows_ref, rows_hbm, rows_sem)
    gone.start()
    for one in arriving:
        one.wait()
    for f in range(frames):
        xt_ref[:, f * tokens : (f + 1) * tokens] = x_ref[f].T
    leaving = copy(xt_ref, xt_hbm, xt_sem)
    leaving.start()
    leaving.wait()
    moved.wait()
    gone.wait()


def backward_kernel(
    bits, clip_count, token_count, me_ref,
    h_hbm, xt_hbm, rows_hbm, ag_ref, part_ref,
    d_hbm, both_ref, loss_ref,
    right_ref, xt_ref, d_ref, grad_ref, h_ref, rows_ref, xt_sem, d_sem, h_sem, rows_sem,
):
    frames, tokens, width = h_hbm.shape
    h_copies = [copy(h_hbm.at[f], h_ref.at[f], h_sem.at[f]) for f in range(frames)]
    rows_copies = [copy(rows_hbm.at[f], rows_ref.at[f], rows_sem.at[f]) for f in range(frames)]
    for f in range(frames):
        rows_copies[f].start()
        h_copies[f].start()
    arriving = copy(xt_hbm, xt_ref, xt_sem)
    arriving.start()
    leaving = [copy(d_ref.at[f], d_hbm.at[f], d_sem.at[f]) for f in range(frames)]
    core = (me_ref[0] // 2) % 2
    total = jnp.sum(part_ref[...], axis=0, keepdims=True)
    lane = lax.broadcasted_iota(jnp.int32, total.shape, 1)
    mean = jnp.where(lane < bits, total / token_count, 0.5)
    lean = jnp.log((1.0 - mean) / mean)
    entropy = -mean * jnp.log(mean) - (1.0 - mean) * jnp.log(1.0 - mean)
    term = jnp.where(lane < bits, -0.1 * entropy, jnp.where(lane == bits, total / token_count, 0.0))
    loss_ref[...] = jnp.sum(term, axis=1, keepdims=True)
    lean = diagonal(lean, ROWS) * 0.05
    high = ag_ref[:ROWS]
    low = ag_ref[ROWS:]
    right_ref[...] = jnp.concatenate(
        [high, high, low, jnp.zeros((LANES - 3 * ROWS, width), BF16)], axis=0
    )
    step = 256
    for f in range(frames):
        for other in {0: [0], 1: range(1, frames)}.get(f, []):
            rows_copies[other].wait()
            h_copies[other].wait()
        u = (rows_ref[f, 0] - rows_ref[f, 1] * lean) * (1.0 / clip_count)
        u_hi, u_lo = hi_lo(u)
        centres = jnp.sum(u * rows_ref[f, 2], axis=0, keepdims=True)
        centres = jnp.broadcast_to(centres, (8, tokens)).T
        spare = jnp.zeros((LANES - 3 * ROWS, tokens), BF16)
        left = jnp.concatenate([u_hi, u_lo, u_hi, spare], axis=0).T
        for start in range(0, tokens, step):
            piece = left[start : start + step]
            rows = slice(start, start + step)
            centre = jnp.broadcast_to(centres[rows, :1], (step, 2 * LANES))
            for col in range(0, width, 2 * LANES):
                cols = slice(col, col + 2 * LANES)
                out = jnp.dot(piece, right_ref[:, cols], preferred_element_type=F32)
                d_ref[f, rows, cols] = (out - centre * h_ref[f, rows, cols].astype(F32)).astype(BF16)
        leaving[f].start()
    block = both_ref.shape[2]
    group = 8 * block
    arriving.wait()
    for k in range(3):
        count = (frames - k) * tokens
        d_part = d_ref[k:].reshape(count, width)
        base = k * width
        grad_ref[base : base + width, :] = jnp.dot(xt_ref[:, :count], d_part, preferred_element_type=F32).astype(BF16)
    for k in range(3):
        base = k * width
        row = base
        while row < base + width:
            stop = min((row // block + 1) * block, base + width)
            half, within = divmod(row, 2 * group)
            owner, inside = divmod(within, group)
            slot, offset = divmod(inside, block)
            where = core if owner == 0 else 1 - core
            both_ref[where, slot * 2 + half, offset : offset + stop - row, :] = grad_ref[row:stop, :]
            row = stop
    for one in leaving:
        one.wait()


def input_kernel(
    me_ref, d_hbm, w_hbm, m_hbm, v_hbm,
    out_hbm, mh_ref, vh_ref,
    w_ref, out_ref, d_ref, w_sem, keep_sem, out_sem, d_sem,
):
    frames, tokens, width = d_hbm.shape
    batch, _, sites, _ = out_hbm.shape
    w_copies = [
        copy(w_hbm.at[pl.ds(k * width, width)], w_ref.at[pl.ds(k * width, width)], w_sem.at[k]) for k in range(3)
    ]
    side_rows = mh_ref.shape[0]
    near = pl.ds(pl.multiple_of((me_ref[0] // 2) % 2 * side_rows, side_rows), side_rows)
    kept = [copy(m_hbm.at[near], mh_ref, keep_sem.at[0]), copy(v_hbm.at[near], vh_ref, keep_sem.at[1])]
    d_copies = [copy(d_hbm.at[f], d_ref.at[f], d_sem.at[f]) for f in range(frames)]
    for i in range(frames):
        d_copies[frames - 1 - i].start()
        if i < 3:
            w_copies[i].start()
    for one in kept:
        one.start()
    sent = []
    for f in range(frames - 1, -1, -1):
        if frames - 1 - f < 3:
            w_copies[frames - 1 - f].wait()
        d_copies[f].wait()
        total = d_ref[f].astype(F32)
        for k in range(min(3, frames - f)):
            total = total + lax.dot_general(
                d_ref[f + k], w_ref[k * width : (k + 1) * width, :], NT, preferred_element_type=F32
            )
        out_ref[f] = total.astype(BF16)
        for c in range(batch):
            one = copy(out_ref.at[f, pl.ds(c * sites, sites)], out_hbm.at[c, f], out_sem.at[f, c])
            one.start()
            sent.append(one)
    for one in kept + sent:
        one.wait()


def moments(first, second, grad):
    return 0.9 * first + 0.1 * grad, 0.99 * second + 0.01 * grad * grad


def stepped(weight, first_out, second_out):
    return (weight - 0.001 * first_out / (jnp.sqrt(second_out) + 1e-08)).astype(BF16)


def block_kernel(me_ref, parts_ref, w_hbm, mh_ref, vh_ref, send_ref, w_ref, w_sem):
    me = me_ref[0]
    half = me % 2
    core = (me // 2) % 2
    slot = (me // 64) * 2 + (me // 4) % 2
    block = parts_ref.shape[1]
    side_rows = mh_ref.shape[0]
    rows = pl.ds(pl.multiple_of(slot * block, block), block)
    start = half * 2 * side_rows + core * side_rows + slot * block
    arriving = copy(w_hbm.at[pl.ds(pl.multiple_of(start, block), block)], w_ref, w_sem)
    arriving.start()
    grad = jnp.sum(parts_ref[...].astype(F32), axis=0).astype(BF16)
    first_out, second_out = moments(mh_ref[rows, :], vh_ref[rows, :], grad.astype(F32))
    arriving.wait()
    new = stepped(w_ref[...].astype(F32), first_out, second_out)
    for d in range(0, send_ref.shape[0], 2):
        send_ref[d + half] = grad
        send_ref[d + 1 - half] = new


def final_kernel(side, me_ref, blocks_ref, w_in, mh_ref, vh_ref, *refs):
    half = me_ref[0] % 2
    core = (me_ref[0] // 2) % 2
    owner = core if side == 0 else 1 - core
    slots, block, width = blocks_ref.shape
    side_rows = mh_ref.shape[0]
    owned = 2 * side_rows
    start = pl.multiple_of(owner * side_rows, side_rows)
    pending = []
    if side == 0:
        m_hbm, v_hbm, new_hbm, first_hbm, second_hbm, w_next, m_next, v_next = refs[:8]
        new_ref, first_ref, second_ref, w_ref, sem, other_sem, w_sem = refs[8:]
        other = pl.ds(pl.multiple_of((1 - owner) * side_rows, side_rows), side_rows)
        other_w = pl.ds(pl.multiple_of(half * owned + (1 - owner) * side_rows, side_rows), side_rows)
        own_w = pl.ds(pl.multiple_of(half * owned + start, side_rows), side_rows)
        near_w = copy(w_in.at[own_w], w_ref, w_sem.at[0])
        near_w.start()
        pending = [
            copy(w_in.at[other_w], w_next, w_sem.at[1]),
            copy(m_hbm.at[other], m_next, w_sem.at[2]),
            copy(v_hbm.at[other], v_next, w_sem.at[3]),
        ]
        for one in pending:
            one.start()
    else:
        new_hbm, first_hbm, second_hbm, new_ref, first_ref, second_ref, sem, other_sem = refs[3:]
        w_ref = w_in
    sent = []
    for slot in range(slots // 2):
        peer = pl.multiple_of((1 - half) * owned + start + slot * block, block)
        sent.append(copy(blocks_ref.at[slot * 2 + 1 - half], new_hbm.at[pl.ds(peer, block)], other_sem.at[slot]))
        sent[-1].start()
    per = 2
    rows = per * block
    chunks = slots // 2 // per

    def first_part(chunk):
        for slot in range(chunk * per, (chunk + 1) * per):
            here = slice(slot * block, (slot + 1) * block)
            grad = blocks_ref[slot * 2 + half].astype(F32)
            first_out, second_out = moments(mh_ref[here, :], vh_ref[here, :], grad)
            first_ref[here, :] = first_out
            second_ref[here, :] = second_out
            if side == 1:
                new_ref[here, :] = stepped(w_ref[here, :].astype(F32), first_out, second_out)
        far = pl.ds(pl.multiple_of(start + chunk * rows, rows), rows)
        for i, (source, target) in enumerate([(first_ref, first_hbm), (second_ref, second_hbm)]):
            one = copy(source.at[pl.ds(chunk * rows, rows)], target.at[far], sem.at[chunk, i])
            one.start()
            sent.append(one)

    def second_part(chunk):
        for slot in range(chunk * per, (chunk + 1) * per) if side == 0 else ():
            here = slice(slot * block, (slot + 1) * block)
            new_ref[here, :] = stepped(w_ref[here, :].astype(F32), first_ref[here, :], second_ref[here, :])
        mine = pl.ds(pl.multiple_of(half * owned + start + chunk * rows, rows), rows)
        one = copy(new_ref.at[pl.ds(chunk * rows, rows)], new_hbm.at[mine], sem.at[chunk, 2])
        one.start()
        sent.append(one)

    for chunk in range(chunks):
        first_part(chunk)
        if side == 1:
            second_part(chunk)
    if side == 0:
        near_w.wait()
        for chunk in range(chunks):
            second_part(chunk)
    for one in sent + pending:
        one.wait()


SCALAR = pl.BlockSpec(memory_space=pltpu.SMEM)
NEAR = pl.BlockSpec(memory_space=pltpu.VMEM)
FAR = pl.BlockSpec(memory_space=pltpu.HBM)
DMA = pltpu.SemaphoreType.DMA
PARAMS = pltpu.CompilerParams(vmem_limit_bytes=32 * 1024 * 1024)


def local(value):
    return pltpu.with_memory_space_constraint(value, pltpu.VMEM)


def remote(value):
    return pltpu.with_memory_space_constraint(value, pltpu.HBM)


def run_forward(me, clips, weight, proj, gain, code_bias, rotation, cotangent, devices):
    batch, frames, sites, width = clips.shape
    tokens = batch * sites
    rows = (frames, ROWS, tokens)
    outs = [
        pltpu.VMEM((frames, tokens, width), BF16), pltpu.VMEM(rows, F32), pltpu.VMEM((frames, 8, tokens), F32),
        pltpu.VMEM((ROWS, LANES), F32), pltpu.VMEM(rows, F32),
        pltpu.VMEM((2 * ROWS, width), BF16), pltpu.VMEM((devices, LANES), F32),
    ]
    return pl.pallas_call(
        forward_kernel,
        in_specs=[SCALAR] + [FAR] * 7,
        out_specs=[NEAR] * 7,
        out_shape=outs,
        scratch_shapes=[
            pltpu.VMEM((frames, tokens, width), BF16), pltpu.VMEM(weight.shape, BF16),
            pltpu.VMEM((ROWS, width), F32),
            *[pltpu.VMEM(a.shape, a.dtype) for a in (proj, gain, code_bias, rotation, cotangent)],
            DMA((frames, batch)), DMA((3,)), DMA((5,)),
        ],
        compiler_params=PARAMS,
        name="forward",
    )(me, *[remote(a) for a in (clips, weight, proj, gain, code_bias, rotation, cotangent)])


def run_window(clips, hidden, raw, inv, bias, cot):
    batch, frames, sites, width = clips.shape
    tokens = batch * sites
    return pl.pallas_call(
        window_kernel,
        in_specs=[FAR] + [NEAR] * 5,
        out_specs=[FAR] * 3,
        out_shape=[
            pltpu.HBM(hidden.shape, BF16), pltpu.HBM((width, frames * tokens), BF16),
            pltpu.HBM((frames, 3, *raw.shape[1:]), F32),
        ],
        scratch_shapes=[
            pltpu.VMEM((frames, tokens, width), BF16), pltpu.VMEM((width, frames * tokens), BF16),
            pltpu.VMEM((frames, 3, *raw.shape[1:]), F32), DMA((frames, batch)), DMA(()), DMA(()), DMA(()),
        ],
        compiler_params=PARAMS,
        name="window",
    )(remote(clips), *[local(a) for a in (hidden, raw, inv, bias, cot)])


def run_backward(bits, clip_count, token_count, me, saved, ag, parts, row_count):
    width = saved[0].shape[2]
    both = (2, 16, row_count // 32, width)
    return pl.pallas_call(
        functools.partial(backward_kernel, bits, clip_count, token_count),
        in_specs=[SCALAR] + [FAR] * 3 + [NEAR] * 2,
        out_specs=[FAR] + [NEAR] * 2,
        out_shape=[
            pltpu.HBM(saved[0].shape, BF16), pltpu.VMEM(both, BF16),
            jax.ShapeDtypeStruct((1, 1), F32),
        ],
        scratch_shapes=[
            pltpu.VMEM((LANES, width), BF16), pltpu.VMEM(saved[1].shape, BF16), pltpu.VMEM(saved[0].shape, BF16),
            pltpu.VMEM((row_count, width), BF16), pltpu.VMEM(saved[0].shape, BF16),
            pltpu.VMEM(saved[2].shape, F32),
            DMA(()), *[DMA((saved[0].shape[0],))] * 3,
        ],
        compiler_params=PARAMS,
        name="backward",
    )(me, *[remote(a) for a in saved], local(ag), local(parts))


def run_input(me, d_conv, weight, first, second, shape):
    batch, frames = shape[:2]
    owned = (first.shape[0] // 2, first.shape[1])
    return pl.pallas_call(
        input_kernel,
        in_specs=[SCALAR] + [FAR] * 4,
        out_specs=[FAR, NEAR, NEAR],
        out_shape=[
            pltpu.HBM(shape, BF16),
            pltpu.VMEM(owned, F32), pltpu.VMEM(owned, F32),
        ],
        scratch_shapes=[
            pltpu.VMEM(weight.shape, BF16), pltpu.VMEM(d_conv.shape, BF16), pltpu.VMEM(d_conv.shape, BF16),
            DMA((3,)), DMA((2,)), DMA((frames, batch)), DMA((frames,)),
        ],
        compiler_params=PARAMS,
        name="input_grad",
    )(me, *[remote(a) for a in (d_conv, weight, first, second)])


def run_block(me, parts, weight, kept):
    send = (16, *parts.shape[1:])
    return pl.pallas_call(
        block_kernel,
        in_specs=[SCALAR, NEAR, FAR, NEAR, NEAR],
        out_specs=NEAR,
        out_shape=pltpu.VMEM(send, BF16),
        scratch_shapes=[pltpu.VMEM(parts.shape[1:], BF16), DMA(())],
        compiler_params=PARAMS,
        name="owner_step",
    )(me, local(parts), remote(weight), *[local(a) for a in kept])


def run_near(me, blocks, weight, first, second, kept):
    owned, width = first.shape
    half = (owned // 2, width)
    return pl.pallas_call(
        functools.partial(final_kernel, 0),
        in_specs=[SCALAR, NEAR, FAR, NEAR, NEAR, FAR, FAR],
        out_specs=[FAR] * 3 + [NEAR] * 3,
        out_shape=[
            pltpu.HBM(weight.shape, BF16), pltpu.HBM(first.shape, F32), pltpu.HBM(first.shape, F32),
            pltpu.VMEM(half, BF16), pltpu.VMEM(half, F32), pltpu.VMEM(half, F32),
        ],
        scratch_shapes=[
            pltpu.VMEM(half, BF16), pltpu.VMEM(half, F32), pltpu.VMEM(half, F32), pltpu.VMEM(half, BF16),
            DMA((4, 3)), DMA((8,)), DMA((4,)),
        ],
        compiler_params=PARAMS,
        name="final_near",
    )(me, local(blocks), remote(weight), *[local(a) for a in kept], remote(first), remote(second))


def run_far(me, blocks, saved, carried):
    half = saved[0].shape
    return pl.pallas_call(
        functools.partial(final_kernel, 1),
        in_specs=[SCALAR] + [NEAR] * 4 + [FAR] * 3,
        out_specs=[FAR] * 3,
        out_shape=[pltpu.HBM(a.shape, a.dtype) for a in carried],
        scratch_shapes=[
            pltpu.VMEM(half, BF16), pltpu.VMEM(half, F32), pltpu.VMEM(half, F32), DMA((4, 3)), DMA((8,)),
        ],
        input_output_aliases={5 + i: i for i in range(3)},
        compiler_params=PARAMS,
        name="final_far",
    )(me, *[local(a) for a in (blocks, *saved)], *[remote(a) for a in carried])


def spread(value, axes):
    return lax.all_to_all(value, axes, 0, 0, tiled=True)


def swapped(value):
    return lax.ppermute(value, "core", [(0, 1), (1, 0)])


def on_device(clips, code_grad, conv_weight, norm_gain, proj_weight, code_bias, rotation, first_moment, second_moment):
    bits = code_grad.shape[3]
    devices = lax.axis_size(ALL)
    batch, frames, sites, width = clips.shape
    clip_count = batch * devices
    token_count = clip_count * frames * sites
    me = lax.axis_index(ALL).astype(jnp.int32).reshape(1)
    cotangent = code_grad.transpose(1, 3, 0, 2)
    hidden, raw, inv, bias, cot, ag, stats = run_forward(
        me, clips, conv_weight, proj_weight.T, norm_gain[None, :], code_bias[None, :], rotation, cotangent, devices
    )
    parts = spread(stats, ALL)
    saved = run_window(clips, hidden, raw, inv, bias, cot)
    d_conv, both, loss = run_backward(
        bits, clip_count, token_count, me, saved, ag, parts, conv_weight.shape[0]
    )
    chip = (both[0].astype(F32) + swapped(both[1]).astype(F32)).astype(BF16)
    plane = spread(chip, PLANE)
    input_grad, *kept = run_input(me, d_conv, conv_weight, first_moment, second_moment, clips.shape)
    plane, kept = lax.optimization_barrier((plane, kept))
    column = jnp.sum(plane.astype(F32), axis=0).astype(BF16)
    tower = spread(jnp.broadcast_to(column, (lax.axis_size("z"), *column.shape)), "z")
    near = spread(run_block(me, tower, conv_weight, kept), PLANE)
    far = swapped(near)
    outs = run_near(me, near, conv_weight, first_moment, second_moment, kept)
    new_weight, first_out, second_out = run_far(me, far, outs[3:], outs[:3])
    return new_weight, first_out, second_out, input_grad, loss[0, 0]


def solution(mesh):
    finer = Mesh(mesh.devices.reshape(4, 8, 2, 2, mesh.shape["shard"]), ALL)
    split = P(ALL, None, None, None)
    in_specs = (split, split, P(), P(), P(), P(), P(), P("yl", None), P("yl", None))
    out_specs = (P(), P("yl", None), P("yl", None), split, P())
    return jax.shard_map(on_device, mesh=finer, in_specs=in_specs, out_specs=out_specs, check_vma=False)
```

```python
import functools

import jax
import jax.numpy as jnp
from jax import lax
from jax.experimental import pallas as pl
from jax.experimental.pallas import tpu as pltpu
from jax.sharding import Mesh
from jax.sharding import PartitionSpec as P

ALL = ("x", "zh", "zl", "yh", "core", "yl")
PLANE = ("x", "zl", "yh", "yl")
ROWS = 24
ROW_STEP = 512
COL_STEP = 512
GRAD_STEP = 512
LANES = 128
F32 = jnp.float32
BF16 = jnp.bfloat16
NT = (((1,), (1,)), ((), ()))
TN = (((0,), (0,)), ((), ()))
EXACT = lax.Precision.HIGHEST


def hi_lo(value):
    high = value.astype(BF16)
    return high, (value - high.astype(F32)).astype(BF16)


def diagonal(row, count):
    grid = jnp.broadcast_to(row, (count, row.shape[1]))
    at = lax.broadcasted_iota(jnp.int32, grid.shape, 0)
    to = lax.broadcasted_iota(jnp.int32, grid.shape, 1)
    return jnp.sum(jnp.where(at == to, grid, 0.0), axis=1, keepdims=True)


def lane_groups(value):
    part = value[:, :LANES]
    for g in range(1, value.shape[1] // LANES):
        part = part + value[:, g * LANES : (g + 1) * LANES]
    return part


def copy(source, target, sem):
    return pltpu.make_async_copy(source, target, sem)


def forward_kernel(
    _, x_hbm, w_hbm, proj_hbm, gain_hbm, code_bias_hbm, rotation_hbm, cg_hbm,
    h_ref, raw_ref, inv_ref, bias_ref, cot_ref, ag_ref, stat_ref,
    x_ref, w_ref, map_ref, proj_ref, gain_ref, code_bias_ref, rotation_ref, cg_ref,
    x_sem, w_sem, small_sem,
):
    batch, frames, sites, width = x_hbm.shape
    bits = rotation_ref.shape[0]
    tokens = batch * sites
    pairs = [
        (proj_hbm, proj_ref), (gain_hbm, gain_ref), (code_bias_hbm, code_bias_ref),
        (rotation_hbm, rotation_ref), (cg_hbm, cg_ref),
    ]
    small_copies = [copy(a, b, small_sem.at[i]) for i, (a, b) in enumerate(pairs)]
    for one in small_copies:
        one.start()
    x_copies = [
        [copy(x_hbm.at[c, f], x_ref.at[f, pl.ds(c * sites, sites)], x_sem.at[f, c]) for c in range(batch)]
        for f in range(frames)
    ]
    w_copies = [
        copy(w_hbm.at[pl.ds(k * width, width)], w_ref.at[pl.ds(k * width, width)], w_sem.at[k]) for k in range(3)
    ]
    for f in range(frames):
        for one in x_copies[f]:
            one.start()
        if f < 3:
            w_copies[f].start()
    map_ref[...] = jnp.zeros_like(map_ref)
    cot_ref[...] = jnp.zeros_like(cot_ref)
    for one in small_copies:
        one.wait()
    map_ref[:bits, :] = (
        lax.dot_general(
            rotation_ref[...], proj_ref[...].astype(F32), TN, precision=EXACT, preferred_element_type=F32
        )
        * gain_ref[...]
    )
    row = jnp.dot(code_bias_ref[...], rotation_ref[...], precision=EXACT, preferred_element_type=F32)
    bias = diagonal(jnp.concatenate([row, jnp.zeros((1, LANES - bits), F32)], axis=1), ROWS)
    bias_ref[...] = jnp.broadcast_to(bias, bias_ref.shape)
    high, low = hi_lo(map_ref[...])
    ag_ref[...] = jnp.concatenate([high, low], axis=0)
    ones = jnp.ones((8, LANES), F32)
    total_p = jnp.zeros((ROWS, LANES), F32)
    total_l = jnp.zeros((ROWS, LANES), F32)
    def multiply(f):
        means = []
        for start in range(0, tokens, ROW_STEP):
            rows = slice(start, start + ROW_STEP)
            part = jnp.zeros((ROW_STEP, LANES), F32)
            for first in range(0, width, COL_STEP):
                cols = slice(first, first + COL_STEP)
                hidden = x_ref[f, rows, cols].astype(F32)
                for k in range(min(f, 2) + 1):
                    hidden = hidden + jnp.dot(
                        x_ref[f - k, rows, :], w_ref[k * width : (k + 1) * width, cols], preferred_element_type=F32
                    )
                h_ref[f, rows, cols] = hidden.astype(BF16)
                part = part + lane_groups(hidden * hidden)
            means.append(lax.dot_general(ones, part, NT, preferred_element_type=F32)[:1] / width)
        both = lax.dot_general(ag_ref[...], h_ref[f], NT, preferred_element_type=F32)
        return jnp.concatenate(means, axis=1), both[:ROWS] + both[ROWS:]

    def decide(f, mean, raw):
        inv = lax.rsqrt(mean + 1e-06)
        rotated = raw * inv + bias
        cot_ref[f, :bits, :sites] = cg_ref[f, :, 0, :].astype(F32)
        cot_ref[f, :bits, sites:] = cg_ref[f, :, 1, :].astype(F32)
        cotangent = cot_ref[f]
        small = jnp.exp(-2.0 * jnp.abs(rotated))
        size = (1.0 - small) / (1.0 + small)
        codes = jnp.where(rotated < 0.0, -size, size)
        probs = 0.5 + 0.5 * codes
        logit = 2.0 * rotated
        gap = rotated - codes
        entropy = jnp.maximum(logit, 0.0) + jnp.log(1.0 + small) - logit * probs
        raw_ref[f] = raw
        inv_ref[f] = jnp.broadcast_to(inv, inv_ref.shape[1:])
        return lane_groups(probs), lane_groups(cotangent * codes + 0.25 * gap * gap + 0.1 * entropy)

    def arrive(f):
        for one in x_copies[f]:
            one.wait()
        if f < 3:
            w_copies[f].wait()

    waiting = []
    for f in range(frames):
        arrive(f)
        ready = multiply(f)
        for earlier in waiting:
            sums = decide(*earlier)
            total_p = total_p + sums[0]
            total_l = total_l + sums[1]
        waiting = [(f, *ready)]
    sums = decide(*waiting[0])
    total_p = total_p + sums[0]
    total_l = total_l + sums[1]
    at = lax.broadcasted_iota(jnp.int32, total_p.shape, 0)
    losses = jnp.sum(jnp.where(at < bits, total_l, 0.0), axis=0, keepdims=True)
    table = jnp.where(at < bits, total_p, jnp.where(at == bits, losses, 0.0))
    filled = jnp.concatenate([table, jnp.zeros((LANES - ROWS, LANES), F32)], axis=0)
    row = lax.dot_general(ones, filled, NT, precision=EXACT, preferred_element_type=F32)
    stat_ref[...] = jnp.broadcast_to(row[:1], stat_ref.shape)


def window_kernel(
    x_hbm, h_ref, raw_ref, inv_ref, bias_ref, cot_ref,
    h_hbm, xt_hbm, rows_hbm,
    x_ref, xt_ref, rows_ref, x_sem, xt_sem, h_sem, rows_sem,
):
    batch, frames, sites, width = x_hbm.shape
    tokens = batch * sites
    arriving = [
        copy(x_hbm.at[c, f], x_ref.at[f, pl.ds(c * sites, sites)], x_sem.at[f, c])
        for f in range(frames)
        for c in range(batch)
    ]
    for one in arriving:
        one.start()
    moved = copy(h_ref, h_hbm, h_sem)
    moved.start()
    bias = bias_ref[:, :1]
    for f in range(frames):
        raw = raw_ref[f]
        inv = inv_ref[f][:1]
        rotated = raw * inv + bias
        cotangent = cot_ref[f]
        small = jnp.exp(-2.0 * jnp.abs(rotated))
        size = (1.0 - small) / (1.0 + small)
        codes = jnp.where(rotated < 0.0, -size, size)
        slope = 1.0 - codes * codes
        base = cotangent * slope + 0.5 * (rotated - codes) * (1.0 - slope) - 0.1 * rotated * slope
        rows_ref[f, 0] = base * inv
        rows_ref[f, 1] = slope * inv
        rows_ref[f, 2] = raw * (inv * inv) / width
    gone = copy(rows_ref, rows_hbm, rows_sem)
    gone.start()
    for one in arriving:
        one.wait()
    for f in range(frames):
        xt_ref[:, f * tokens : (f + 1) * tokens] = x_ref[f].T
    leaving = copy(xt_ref, xt_hbm, xt_sem)
    leaving.start()
    leaving.wait()
    moved.wait()
    gone.wait()


def backward_kernel(
    bits, clip_count, token_count, me_ref,
    h_hbm, xt_hbm, rows_hbm, ag_ref, part_ref,
    d_hbm, both_ref, loss_ref,
    right_ref, xt_ref, d_ref, grad_ref, h_ref, rows_ref, xt_sem, d_sem, h_sem, rows_sem,
):
    frames, tokens, width = h_hbm.shape
    h_copies = [copy(h_hbm.at[f], h_ref.at[f], h_sem.at[f]) for f in range(frames)]
    rows_copies = [copy(rows_hbm.at[f], rows_ref.at[f], rows_sem.at[f]) for f in range(frames)]
    for f in range(frames):
        rows_copies[f].start()
        h_copies[f].start()
    arriving = copy(xt_hbm, xt_ref, xt_sem)
    arriving.start()
    leaving = [copy(d_ref.at[f], d_hbm.at[f], d_sem.at[f]) for f in range(frames)]
    core = (me_ref[0] // 2) % 2
    total = jnp.sum(part_ref[...], axis=0, keepdims=True)
    lane = lax.broadcasted_iota(jnp.int32, total.shape, 1)
    mean = jnp.where(lane < bits, total / token_count, 0.5)
    lean = jnp.log((1.0 - mean) / mean)
    entropy = -mean * jnp.log(mean) - (1.0 - mean) * jnp.log(1.0 - mean)
    term = jnp.where(lane < bits, -0.1 * entropy, jnp.where(lane == bits, total / token_count, 0.0))
    loss_ref[...] = jnp.sum(term, axis=1, keepdims=True)
    lean = diagonal(lean, ROWS) * 0.05
    high = ag_ref[:ROWS]
    low = ag_ref[ROWS:]
    right_ref[...] = jnp.concatenate(
        [high, high, low, jnp.zeros((LANES - 3 * ROWS, width), BF16)], axis=0
    )
    step = 256
    for f in range(frames):
        for other in {0: [0], 1: range(1, frames)}.get(f, []):
            rows_copies[other].wait()
            h_copies[other].wait()
        u = (rows_ref[f, 0] - rows_ref[f, 1] * lean) * (1.0 / clip_count)
        u_hi, u_lo = hi_lo(u)
        centres = jnp.sum(u * rows_ref[f, 2], axis=0, keepdims=True)
        centres = jnp.broadcast_to(centres, (8, tokens)).T
        spare = jnp.zeros((LANES - 3 * ROWS, tokens), BF16)
        left = jnp.concatenate([u_hi, u_lo, u_hi, spare], axis=0).T
        for start in range(0, tokens, step):
            piece = left[start : start + step]
            rows = slice(start, start + step)
            centre = jnp.broadcast_to(centres[rows, :1], (step, 2 * LANES))
            for col in range(0, width, 2 * LANES):
                cols = slice(col, col + 2 * LANES)
                out = jnp.dot(piece, right_ref[:, cols], preferred_element_type=F32)
                d_ref[f, rows, cols] = (out - centre * h_ref[f, rows, cols].astype(F32)).astype(BF16)
        leaving[f].start()
    block = both_ref.shape[2]
    group = 8 * block
    arriving.wait()
    for k in range(3):
        count = (frames - k) * tokens
        d_part = d_ref[k:].reshape(count, width)
        base = k * width
        grad_ref[base : base + width, :] = jnp.dot(xt_ref[:, :count], d_part, preferred_element_type=F32).astype(BF16)
    for k in range(3):
        base = k * width
        row = base
        while row < base + width:
            stop = min((row // block + 1) * block, base + width)
            half, within = divmod(row, 2 * group)
            owner, inside = divmod(within, group)
            slot, offset = divmod(inside, block)
            where = core if owner == 0 else 1 - core
            for z in range(2):
                index = (slot // 2) * 8 + z * 4 + (slot % 2) * 2 + half
                cols = slice(z * width // 2, (z + 1) * width // 2)
                both_ref[where, index, offset : offset + stop - row, :] = grad_ref[row:stop, cols]
            row = stop
    for one in leaving:
        one.wait()


def input_kernel(
    me_ref, d_hbm, w_hbm, m_hbm, v_hbm,
    out_hbm, mh_ref, vh_ref,
    w_ref, out_ref, d_ref, w_sem, keep_sem, out_sem, d_sem,
):
    frames, tokens, width = d_hbm.shape
    batch, _, sites, _ = out_hbm.shape
    w_copies = [
        copy(w_hbm.at[pl.ds(k * width, width)], w_ref.at[pl.ds(k * width, width)], w_sem.at[k]) for k in range(3)
    ]
    side_rows = mh_ref.shape[0]
    near = pl.ds(pl.multiple_of((me_ref[0] // 2) % 2 * side_rows, side_rows), side_rows)
    kept = [copy(m_hbm.at[near], mh_ref, keep_sem.at[0]), copy(v_hbm.at[near], vh_ref, keep_sem.at[1])]
    d_copies = [copy(d_hbm.at[f], d_ref.at[f], d_sem.at[f]) for f in range(frames)]
    for i in range(frames):
        d_copies[frames - 1 - i].start()
        if i < 3:
            w_copies[i].start()
    for one in kept:
        one.start()
    sent = []
    for f in range(frames - 1, -1, -1):
        if frames - 1 - f < 3:
            w_copies[frames - 1 - f].wait()
        d_copies[f].wait()
        total = d_ref[f].astype(F32)
        for k in range(min(3, frames - f)):
            total = total + lax.dot_general(
                d_ref[f + k], w_ref[k * width : (k + 1) * width, :], NT, preferred_element_type=F32
            )
        out_ref[f] = total.astype(BF16)
        for c in range(batch):
            one = copy(out_ref.at[f, pl.ds(c * sites, sites)], out_hbm.at[c, f], out_sem.at[f, c])
            one.start()
            sent.append(one)
    for one in kept + sent:
        one.wait()


def moments(first, second, grad):
    return 0.9 * first + 0.1 * grad, 0.99 * second + 0.01 * grad * grad


def stepped(weight, first_out, second_out):
    return (weight - 0.001 * first_out / (jnp.sqrt(second_out) + 1e-08)).astype(BF16)


def block_kernel(me_ref, parts_ref, w_hbm, mh_ref, vh_ref, send_ref, w_ref, w_sem):
    me = me_ref[0]
    half = me % 2
    core = (me // 2) % 2
    slot = (me // 64) * 2 + (me // 4) % 2
    z_low = (me // 8) % 2
    _, block, width = parts_ref.shape
    side_rows = mh_ref.shape[0]
    rows = pl.ds(pl.multiple_of(slot * block, block), block)
    start = pl.multiple_of(half * 2 * side_rows + core * side_rows + slot * block, block)
    arriving = copy(w_hbm.at[pl.ds(start, block), pl.ds(pl.multiple_of(z_low * width, width), width)], w_ref, w_sem)
    arriving.start()
    grad = jnp.sum(parts_ref[...].astype(F32), axis=0).astype(BF16)
    first = jnp.where(z_low == 0, mh_ref[rows, :width], mh_ref[rows, width:])
    second = jnp.where(z_low == 0, vh_ref[rows, :width], vh_ref[rows, width:])
    first_out, second_out = moments(first, second, grad.astype(F32))
    arriving.wait()
    new = stepped(w_ref[...].astype(F32), first_out, second_out)
    for d in range(0, send_ref.shape[0], 2):
        send_ref[d + half] = grad
        send_ref[d + 1 - half] = new


def final_kernel(side, me_ref, blocks_ref, w_in, mh_ref, vh_ref, *refs):
    half = me_ref[0] % 2
    core = (me_ref[0] // 2) % 2
    owner = core if side == 0 else 1 - core
    count, block, part_width = blocks_ref.shape
    slots = count // 2
    side_rows = mh_ref.shape[0]
    owned = 2 * side_rows
    start = pl.multiple_of(owner * side_rows, side_rows)
    pending = []
    if side == 0:
        m_hbm, v_hbm, new_hbm, first_hbm, second_hbm, w_next, m_next, v_next = refs[:8]
        new_ref, first_ref, second_ref, w_ref, sem, other_sem, w_sem = refs[8:]
        other = pl.ds(pl.multiple_of((1 - owner) * side_rows, side_rows), side_rows)
        other_w = pl.ds(pl.multiple_of(half * owned + (1 - owner) * side_rows, side_rows), side_rows)
        own_w = pl.ds(pl.multiple_of(half * owned + start, side_rows), side_rows)
        near_w = copy(w_in.at[own_w], w_ref, w_sem.at[0])
        near_w.start()
        pending = [
            copy(w_in.at[other_w], w_next, w_sem.at[1]),
            copy(m_hbm.at[other], m_next, w_sem.at[2]),
            copy(v_hbm.at[other], v_next, w_sem.at[3]),
        ]
        for one in pending:
            one.start()
    else:
        new_hbm, first_hbm, second_hbm, new_ref, first_ref, second_ref, sem, other_sem = refs[3:]
        w_ref = w_in
    sent = []
    for slot in range(slots // 2):
        peer = pl.ds(pl.multiple_of((1 - half) * owned + start + slot * block, block), block)
        for z in range(2):
            source = blocks_ref.at[(slot // 2) * 8 + z * 4 + (slot % 2) * 2 + 1 - half]
            cols = pl.ds(z * part_width, part_width)
            sent.append(copy(source, new_hbm.at[peer, cols], other_sem.at[slot, z]))
            sent[-1].start()
    per = 2
    rows = per * block
    chunks = slots // 2 // per

    def first_part(chunk):
        for slot in range(chunk * per, (chunk + 1) * per):
            here = slice(slot * block, (slot + 1) * block)
            index = (slot // 2) * 8 + (slot % 2) * 2 + half
            grad = jnp.concatenate([blocks_ref[index], blocks_ref[index + 4]], axis=1).astype(F32)
            first_out, second_out = moments(mh_ref[here, :], vh_ref[here, :], grad)
            first_ref[here, :] = first_out
            second_ref[here, :] = second_out
            if side == 1:
                new_ref[here, :] = stepped(w_ref[here, :].astype(F32), first_out, second_out)
        far = pl.ds(pl.multiple_of(start + chunk * rows, rows), rows)
        for i, (source, target) in enumerate([(first_ref, first_hbm), (second_ref, second_hbm)]):
            one = copy(source.at[pl.ds(chunk * rows, rows)], target.at[far], sem.at[chunk, i])
            one.start()
            sent.append(one)

    def second_part(chunk):
        for slot in range(chunk * per, (chunk + 1) * per) if side == 0 else ():
            here = slice(slot * block, (slot + 1) * block)
            new_ref[here, :] = stepped(w_ref[here, :].astype(F32), first_ref[here, :], second_ref[here, :])
        mine = pl.ds(pl.multiple_of(half * owned + start + chunk * rows, rows), rows)
        one = copy(new_ref.at[pl.ds(chunk * rows, rows)], new_hbm.at[mine], sem.at[chunk, 2])
        one.start()
        sent.append(one)

    for chunk in range(chunks):
        first_part(chunk)
        if side == 1:
            second_part(chunk)
    if side == 0:
        near_w.wait()
        for chunk in range(chunks):
            second_part(chunk)
    for one in sent + pending:
        one.wait()


SCALAR = pl.BlockSpec(memory_space=pltpu.SMEM)
NEAR = pl.BlockSpec(memory_space=pltpu.VMEM)
FAR = pl.BlockSpec(memory_space=pltpu.HBM)
DMA = pltpu.SemaphoreType.DMA
PARAMS = pltpu.CompilerParams(vmem_limit_bytes=32 * 1024 * 1024)


def local(value):
    return pltpu.with_memory_space_constraint(value, pltpu.VMEM)


def remote(value):
    return pltpu.with_memory_space_constraint(value, pltpu.HBM)


def run_forward(me, clips, weight, proj, gain, code_bias, rotation, cotangent, devices):
    batch, frames, sites, width = clips.shape
    tokens = batch * sites
    rows = (frames, ROWS, tokens)
    outs = [
        pltpu.VMEM((frames, tokens, width), BF16), pltpu.VMEM(rows, F32), pltpu.VMEM((frames, 8, tokens), F32),
        pltpu.VMEM((ROWS, LANES), F32), pltpu.VMEM(rows, F32),
        pltpu.VMEM((2 * ROWS, width), BF16), pltpu.VMEM((devices, LANES), F32),
    ]
    return pl.pallas_call(
        forward_kernel,
        in_specs=[SCALAR] + [FAR] * 7,
        out_specs=[NEAR] * 7,
        out_shape=outs,
        scratch_shapes=[
            pltpu.VMEM((frames, tokens, width), BF16), pltpu.VMEM(weight.shape, BF16),
            pltpu.VMEM((ROWS, width), F32),
            *[pltpu.VMEM(a.shape, a.dtype) for a in (proj, gain, code_bias, rotation, cotangent)],
            DMA((frames, batch)), DMA((3,)), DMA((5,)),
        ],
        compiler_params=PARAMS,
        name="forward",
    )(me, *[remote(a) for a in (clips, weight, proj, gain, code_bias, rotation, cotangent)])


def run_window(clips, hidden, raw, inv, bias, cot):
    batch, frames, sites, width = clips.shape
    tokens = batch * sites
    return pl.pallas_call(
        window_kernel,
        in_specs=[FAR] + [NEAR] * 5,
        out_specs=[FAR] * 3,
        out_shape=[
            pltpu.HBM(hidden.shape, BF16), pltpu.HBM((width, frames * tokens), BF16),
            pltpu.HBM((frames, 3, *raw.shape[1:]), F32),
        ],
        scratch_shapes=[
            pltpu.VMEM((frames, tokens, width), BF16), pltpu.VMEM((width, frames * tokens), BF16),
            pltpu.VMEM((frames, 3, *raw.shape[1:]), F32), DMA((frames, batch)), DMA(()), DMA(()), DMA(()),
        ],
        compiler_params=PARAMS,
        name="window",
    )(remote(clips), *[local(a) for a in (hidden, raw, inv, bias, cot)])


def run_backward(bits, clip_count, token_count, me, saved, ag, parts, row_count):
    width = saved[0].shape[2]
    both = (2, 32, row_count // 32, width // 2)
    return pl.pallas_call(
        functools.partial(backward_kernel, bits, clip_count, token_count),
        in_specs=[SCALAR] + [FAR] * 3 + [NEAR] * 2,
        out_specs=[FAR] + [NEAR] * 2,
        out_shape=[
            pltpu.HBM(saved[0].shape, BF16), pltpu.VMEM(both, BF16),
            jax.ShapeDtypeStruct((1, 1), F32),
        ],
        scratch_shapes=[
            pltpu.VMEM((LANES, width), BF16), pltpu.VMEM(saved[1].shape, BF16), pltpu.VMEM(saved[0].shape, BF16),
            pltpu.VMEM((row_count, width), BF16), pltpu.VMEM(saved[0].shape, BF16),
            pltpu.VMEM(saved[2].shape, F32),
            DMA(()), *[DMA((saved[0].shape[0],))] * 3,
        ],
        compiler_params=PARAMS,
        name="backward",
    )(me, *[remote(a) for a in saved], local(ag), local(parts))


def run_input(me, d_conv, weight, first, second, shape):
    batch, frames = shape[:2]
    owned = (first.shape[0] // 2, first.shape[1])
    return pl.pallas_call(
        input_kernel,
        in_specs=[SCALAR] + [FAR] * 4,
        out_specs=[FAR, NEAR, NEAR],
        out_shape=[
            pltpu.HBM(shape, BF16),
            pltpu.VMEM(owned, F32), pltpu.VMEM(owned, F32),
        ],
        scratch_shapes=[
            pltpu.VMEM(weight.shape, BF16), pltpu.VMEM(d_conv.shape, BF16), pltpu.VMEM(d_conv.shape, BF16),
            DMA((3,)), DMA((2,)), DMA((frames, batch)), DMA((frames,)),
        ],
        compiler_params=PARAMS,
        name="input_grad",
    )(me, *[remote(a) for a in (d_conv, weight, first, second)])


def run_block(me, parts, weight, kept):
    send = (32, *parts.shape[1:])
    return pl.pallas_call(
        block_kernel,
        in_specs=[SCALAR, NEAR, FAR, NEAR, NEAR],
        out_specs=NEAR,
        out_shape=pltpu.VMEM(send, BF16),
        scratch_shapes=[pltpu.VMEM(parts.shape[1:], BF16), DMA(())],
        compiler_params=PARAMS,
        name="owner_step",
    )(me, local(parts), remote(weight), *[local(a) for a in kept])


def run_near(me, blocks, weight, first, second, kept):
    owned, width = first.shape
    half = (owned // 2, width)
    return pl.pallas_call(
        functools.partial(final_kernel, 0),
        in_specs=[SCALAR, NEAR, FAR, NEAR, NEAR, FAR, FAR],
        out_specs=[FAR] * 3 + [NEAR] * 3,
        out_shape=[
            pltpu.HBM(weight.shape, BF16), pltpu.HBM(first.shape, F32), pltpu.HBM(first.shape, F32),
            pltpu.VMEM(half, BF16), pltpu.VMEM(half, F32), pltpu.VMEM(half, F32),
        ],
        scratch_shapes=[
            pltpu.VMEM(half, BF16), pltpu.VMEM(half, F32), pltpu.VMEM(half, F32), pltpu.VMEM(half, BF16),
            DMA((4, 3)), DMA((8, 2)), DMA((4,)),
        ],
        compiler_params=PARAMS,
        name="final_near",
    )(me, local(blocks), remote(weight), *[local(a) for a in kept], remote(first), remote(second))


def run_far(me, blocks, saved, carried):
    half = saved[0].shape
    return pl.pallas_call(
        functools.partial(final_kernel, 1),
        in_specs=[SCALAR] + [NEAR] * 4 + [FAR] * 3,
        out_specs=[FAR] * 3,
        out_shape=[pltpu.HBM(a.shape, a.dtype) for a in carried],
        scratch_shapes=[
            pltpu.VMEM(half, BF16), pltpu.VMEM(half, F32), pltpu.VMEM(half, F32), DMA((4, 3)), DMA((8, 2)),
        ],
        input_output_aliases={5 + i: i for i in range(3)},
        compiler_params=PARAMS,
        name="final_far",
    )(me, *[local(a) for a in (blocks, *saved)], *[remote(a) for a in carried])


def spread(value, axes):
    return lax.all_to_all(value, axes, 0, 0, tiled=True)


def swapped(value):
    return lax.ppermute(value, "core", [(0, 1), (1, 0)])


def on_device(clips, code_grad, conv_weight, norm_gain, proj_weight, code_bias, rotation, first_moment, second_moment):
    bits = code_grad.shape[3]
    devices = lax.axis_size(ALL)
    batch, frames, sites, width = clips.shape
    clip_count = batch * devices
    token_count = clip_count * frames * sites
    me = lax.axis_index(ALL).astype(jnp.int32).reshape(1)
    cotangent = code_grad.transpose(1, 3, 0, 2)
    hidden, raw, inv, bias, cot, ag, stats = run_forward(
        me, clips, conv_weight, proj_weight.T, norm_gain[None, :], code_bias[None, :], rotation, cotangent, devices
    )
    parts = spread(stats, ALL)
    saved = run_window(clips, hidden, raw, inv, bias, cot)
    d_conv, both, loss = run_backward(
        bits, clip_count, token_count, me, saved, ag, parts, conv_weight.shape[0]
    )
    chip = (both[0].astype(F32) + swapped(both[1]).astype(F32)).astype(BF16)
    plane = spread(chip, PLANE)
    input_grad, *kept = run_input(me, d_conv, conv_weight, first_moment, second_moment, clips.shape)
    plane, kept = lax.optimization_barrier((plane, kept))
    column = jnp.sum(plane.astype(F32), axis=0).astype(BF16)
    tower = spread(jnp.broadcast_to(column, (lax.axis_size("zh"), *column.shape)), "zh")
    near = spread(run_block(me, tower, conv_weight, kept), PLANE)
    far = swapped(near)
    outs = run_near(me, near, conv_weight, first_moment, second_moment, kept)
    new_weight, first_out, second_out = run_far(me, far, outs[3:], outs[:3])
    return new_weight, first_out, second_out, input_grad, loss[0, 0]


def solution(mesh):
    finer = Mesh(mesh.devices.reshape(4, 4, 2, 2, 2, mesh.shape["shard"]), ALL)
    split = P(ALL, None, None, None)
    in_specs = (split, split, P(), P(), P(), P(), P(), P("yl", None), P("yl", None))
    out_specs = (P(), P("yl", None), P("yl", None), split, P())
    return jax.shard_map(on_device, mesh=finer, in_specs=in_specs, out_specs=out_specs, check_vma=False)
```

```python
import functools

import jax
import jax.numpy as jnp
from jax import lax
from jax.experimental import pallas as pl
from jax.experimental.pallas import tpu as pltpu
from jax.sharding import Mesh
from jax.sharding import PartitionSpec as P

ALL = ("x", "zh", "zl", "yh", "core", "yl")
PLANE = ("x", "zl", "yh", "yl")
ROWS = 24
ROW_STEP = 512
COL_STEP = 512
GRAD_STEP = 512
LANES = 128
F32 = jnp.float32
BF16 = jnp.bfloat16
NT = (((1,), (1,)), ((), ()))
TN = (((0,), (0,)), ((), ()))
EXACT = lax.Precision.HIGHEST


def hi_lo(value):
    high = value.astype(BF16)
    return high, (value - high.astype(F32)).astype(BF16)


def diagonal(row, count):
    grid = jnp.broadcast_to(row, (count, row.shape[1]))
    at = lax.broadcasted_iota(jnp.int32, grid.shape, 0)
    to = lax.broadcasted_iota(jnp.int32, grid.shape, 1)
    return jnp.sum(jnp.where(at == to, grid, 0.0), axis=1, keepdims=True)


def lane_groups(value):
    part = value[:, :LANES]
    for g in range(1, value.shape[1] // LANES):
        part = part + value[:, g * LANES : (g + 1) * LANES]
    return part


def copy(source, target, sem):
    return pltpu.make_async_copy(source, target, sem)


def forward_kernel(
    _, x_hbm, w_hbm, proj_hbm, gain_hbm, code_bias_hbm, rotation_hbm, cg_hbm,
    h_ref, raw_ref, inv_ref, bias_ref, cot_ref, ag_ref, stat_ref,
    x_ref, w_ref, map_ref, proj_ref, gain_ref, code_bias_ref, rotation_ref, cg_ref,
    x_sem, w_sem, small_sem,
):
    batch, frames, sites, width = x_hbm.shape
    bits = rotation_ref.shape[0]
    tokens = batch * sites
    pairs = [
        (proj_hbm, proj_ref), (gain_hbm, gain_ref), (code_bias_hbm, code_bias_ref),
        (rotation_hbm, rotation_ref), (cg_hbm, cg_ref),
    ]
    small_copies = [copy(a, b, small_sem.at[i]) for i, (a, b) in enumerate(pairs)]
    for one in small_copies:
        one.start()
    x_copies = [
        [copy(x_hbm.at[c, f], x_ref.at[f, pl.ds(c * sites, sites)], x_sem.at[f, c]) for c in range(batch)]
        for f in range(frames)
    ]
    w_copies = [
        copy(w_hbm.at[pl.ds(k * width, width)], w_ref.at[pl.ds(k * width, width)], w_sem.at[k]) for k in range(3)
    ]
    for f in range(frames):
        for one in x_copies[f]:
            one.start()
        if f < 3:
            w_copies[f].start()
    map_ref[...] = jnp.zeros_like(map_ref)
    cot_ref[...] = jnp.zeros_like(cot_ref)
    for one in small_copies:
        one.wait()
    map_ref[:bits, :] = (
        lax.dot_general(
            rotation_ref[...], proj_ref[...].astype(F32), TN, precision=EXACT, preferred_element_type=F32
        )
        * gain_ref[...]
    )
    row = jnp.dot(code_bias_ref[...], rotation_ref[...], precision=EXACT, preferred_element_type=F32)
    bias = diagonal(jnp.concatenate([row, jnp.zeros((1, LANES - bits), F32)], axis=1), ROWS)
    bias_ref[...] = jnp.broadcast_to(bias, bias_ref.shape)
    high, low = hi_lo(map_ref[...])
    ag_ref[...] = jnp.concatenate([high, low], axis=0)
    ones = jnp.ones((8, LANES), F32)
    total_p = jnp.zeros((ROWS, LANES), F32)
    total_l = jnp.zeros((ROWS, LANES), F32)
    def multiply(f):
        means = []
        for start in range(0, tokens, ROW_STEP):
            rows = slice(start, start + ROW_STEP)
            part = jnp.zeros((ROW_STEP, LANES), F32)
            for first in range(0, width, COL_STEP):
                cols = slice(first, first + COL_STEP)
                hidden = x_ref[f, rows, cols].astype(F32)
                for k in range(min(f, 2) + 1):
                    hidden = hidden + jnp.dot(
                        x_ref[f - k, rows, :], w_ref[k * width : (k + 1) * width, cols], preferred_element_type=F32
                    )
                h_ref[f, rows, cols] = hidden.astype(BF16)
                part = part + lane_groups(hidden * hidden)
            means.append(lax.dot_general(ones, part, NT, preferred_element_type=F32)[:1] / width)
        both = lax.dot_general(ag_ref[...], h_ref[f], NT, preferred_element_type=F32)
        return jnp.concatenate(means, axis=1), both[:ROWS] + both[ROWS:]

    def decide(f, mean, raw):
        inv = lax.rsqrt(mean + 1e-06)
        rotated = raw * inv + bias
        cot_ref[f, :bits, :sites] = cg_ref[f, :, 0, :].astype(F32)
        cot_ref[f, :bits, sites:] = cg_ref[f, :, 1, :].astype(F32)
        cotangent = cot_ref[f]
        small = jnp.exp(-2.0 * jnp.abs(rotated))
        size = (1.0 - small) / (1.0 + small)
        codes = jnp.where(rotated < 0.0, -size, size)
        probs = 0.5 + 0.5 * codes
        logit = 2.0 * rotated
        gap = rotated - codes
        entropy = jnp.maximum(logit, 0.0) + jnp.log(1.0 + small) - logit * probs
        raw_ref[f] = raw
        inv_ref[f] = jnp.broadcast_to(inv, inv_ref.shape[1:])
        return lane_groups(probs), lane_groups(cotangent * codes + 0.25 * gap * gap + 0.1 * entropy)

    def arrive(f):
        for one in x_copies[f]:
            one.wait()
        if f < 3:
            w_copies[f].wait()

    waiting = []
    for f in range(frames):
        arrive(f)
        ready = multiply(f)
        for earlier in waiting:
            sums = decide(*earlier)
            total_p = total_p + sums[0]
            total_l = total_l + sums[1]
        waiting = [(f, *ready)]
    sums = decide(*waiting[0])
    total_p = total_p + sums[0]
    total_l = total_l + sums[1]
    at = lax.broadcasted_iota(jnp.int32, total_p.shape, 0)
    losses = jnp.sum(jnp.where(at < bits, total_l, 0.0), axis=0, keepdims=True)
    table = jnp.where(at < bits, total_p, jnp.where(at == bits, losses, 0.0))
    filled = jnp.concatenate([table, jnp.zeros((LANES - ROWS, LANES), F32)], axis=0)
    row = lax.dot_general(ones, filled, NT, precision=EXACT, preferred_element_type=F32)
    stat_ref[...] = jnp.broadcast_to(row[:1], stat_ref.shape)


def window_kernel(
    x_hbm, h_ref, raw_ref, inv_ref, bias_ref, cot_ref,
    h_hbm, xt_hbm, rows_hbm,
    x_ref, xt_ref, rows_ref, x_sem, xt_sem, h_sem, rows_sem,
):
    batch, frames, sites, width = x_hbm.shape
    tokens = batch * sites
    arriving = [
        copy(x_hbm.at[c, f], x_ref.at[f, pl.ds(c * sites, sites)], x_sem.at[f, c])
        for f in range(frames)
        for c in range(batch)
    ]
    for one in arriving:
        one.start()
    moved = copy(h_ref, h_hbm, h_sem)
    moved.start()
    bias = bias_ref[:, :1]
    for f in range(frames):
        raw = raw_ref[f]
        inv = inv_ref[f][:1]
        rotated = raw * inv + bias
        cotangent = cot_ref[f]
        small = jnp.exp(-2.0 * jnp.abs(rotated))
        size = (1.0 - small) / (1.0 + small)
        codes = jnp.where(rotated < 0.0, -size, size)
        slope = 1.0 - codes * codes
        base = cotangent * slope + 0.5 * (rotated - codes) * (1.0 - slope) - 0.1 * rotated * slope
        rows_ref[f, 0] = base * inv
        rows_ref[f, 1] = slope * inv
        rows_ref[f, 2] = raw * (inv * inv) / width
    gone = copy(rows_ref, rows_hbm, rows_sem)
    gone.start()
    for one in arriving:
        one.wait()
    for f in range(frames):
        xt_ref[:, f * tokens : (f + 1) * tokens] = x_ref[f].T
    leaving = copy(xt_ref, xt_hbm, xt_sem)
    leaving.start()
    leaving.wait()
    moved.wait()
    gone.wait()


def backward_kernel(
    bits, clip_count, token_count, me_ref,
    h_hbm, xt_hbm, rows_hbm, ag_ref, part_ref,
    d_hbm, both_ref, loss_ref,
    right_ref, xt_ref, d_ref, grad_ref, h_ref, rows_ref, xt_sem, d_sem, h_sem, rows_sem,
):
    frames, tokens, width = h_hbm.shape
    h_copies = [copy(h_hbm.at[f], h_ref.at[f], h_sem.at[f]) for f in range(frames)]
    rows_copies = [copy(rows_hbm.at[f], rows_ref.at[f], rows_sem.at[f]) for f in range(frames)]
    for f in range(frames):
        rows_copies[f].start()
        h_copies[f].start()
    arriving = copy(xt_hbm, xt_ref, xt_sem)
    arriving.start()
    leaving = [copy(d_ref.at[f], d_hbm.at[f], d_sem.at[f]) for f in range(frames)]
    core = (me_ref[0] // 2) % 2
    total = jnp.sum(part_ref[...], axis=0, keepdims=True)
    lane = lax.broadcasted_iota(jnp.int32, total.shape, 1)
    mean = jnp.where(lane < bits, total / token_count, 0.5)
    lean = jnp.log((1.0 - mean) / mean)
    entropy = -mean * jnp.log(mean) - (1.0 - mean) * jnp.log(1.0 - mean)
    term = jnp.where(lane < bits, -0.1 * entropy, jnp.where(lane == bits, total / token_count, 0.0))
    loss_ref[...] = jnp.sum(term, axis=1, keepdims=True)
    lean = diagonal(lean, ROWS) * 0.05
    high = ag_ref[:ROWS]
    low = ag_ref[ROWS:]
    right_ref[...] = jnp.concatenate(
        [high, high, low, jnp.zeros((LANES - 3 * ROWS, width), BF16)], axis=0
    )
    step = 256
    for f in range(frames):
        for other in {0: [0], 1: range(1, frames)}.get(f, []):
            rows_copies[other].wait()
            h_copies[other].wait()
        u = (rows_ref[f, 0] - rows_ref[f, 1] * lean) * (1.0 / clip_count)
        u_hi, u_lo = hi_lo(u)
        centres = jnp.sum(u * rows_ref[f, 2], axis=0, keepdims=True)
        centres = jnp.broadcast_to(centres, (8, tokens)).T
        spare = jnp.zeros((LANES - 3 * ROWS, tokens), BF16)
        left = jnp.concatenate([u_hi, u_lo, u_hi, spare], axis=0).T
        for start in range(0, tokens, step):
            piece = left[start : start + step]
            rows = slice(start, start + step)
            centre = jnp.broadcast_to(centres[rows, :1], (step, 2 * LANES))
            for col in range(0, width, 2 * LANES):
                cols = slice(col, col + 2 * LANES)
                out = jnp.dot(piece, right_ref[:, cols], preferred_element_type=F32)
                d_ref[f, rows, cols] = (out - centre * h_ref[f, rows, cols].astype(F32)).astype(BF16)
        leaving[f].start()
    block = both_ref.shape[2]
    group = 8 * block
    arriving.wait()
    for k in range(3):
        count = (frames - k) * tokens
        d_part = d_ref[k:].reshape(count, width)
        base = k * width
        grad_ref[base : base + width, :] = jnp.dot(xt_ref[:, :count], d_part, preferred_element_type=F32).astype(BF16)
    for k in range(3):
        base = k * width
        row = base
        while row < base + width:
            stop = min((row // block + 1) * block, base + width)
            half, within = divmod(row, 2 * group)
            owner, inside = divmod(within, group)
            slot, offset = divmod(inside, block)
            where = core if owner == 0 else 1 - core
            for z in range(2):
                index = (slot // 2) * 8 + z * 4 + (slot % 2) * 2 + half
                cols = slice(z * width // 2, (z + 1) * width // 2)
                both_ref[where, index, offset : offset + stop - row, :] = grad_ref[row:stop, cols]
            row = stop
    for one in leaving:
        one.wait()


def input_kernel(
    me_ref, d_hbm, w_hbm, m_hbm, v_hbm,
    out_hbm, mh_ref, vh_ref, wh_ref,
    w_ref, out_ref, d_ref, w_sem, keep_sem, out_sem, d_sem,
):
    frames, tokens, width = d_hbm.shape
    batch, _, sites, _ = out_hbm.shape
    w_copies = [
        copy(w_hbm.at[pl.ds(k * width, width)], w_ref.at[pl.ds(k * width, width)], w_sem.at[k]) for k in range(3)
    ]
    side_rows = mh_ref.shape[0]
    near = pl.ds(pl.multiple_of((me_ref[0] // 2) % 2 * side_rows, side_rows), side_rows)
    near_w = me_ref[0] % 2 * 2 * side_rows + (me_ref[0] // 2) % 2 * side_rows
    near_w = pl.ds(pl.multiple_of(near_w, side_rows), side_rows)
    kept = [
        copy(m_hbm.at[near], mh_ref, keep_sem.at[0]),
        copy(v_hbm.at[near], vh_ref, keep_sem.at[1]),
        copy(w_hbm.at[near_w], wh_ref, keep_sem.at[2]),
    ]
    d_copies = [copy(d_hbm.at[f], d_ref.at[f], d_sem.at[f]) for f in range(frames)]
    for i in range(frames):
        d_copies[frames - 1 - i].start()
        if i < 3:
            w_copies[i].start()
    for one in kept:
        one.start()
    sent = []
    for f in range(frames - 1, -1, -1):
        if frames - 1 - f < 3:
            w_copies[frames - 1 - f].wait()
        d_copies[f].wait()
        total = d_ref[f].astype(F32)
        for k in range(min(3, frames - f)):
            total = total + lax.dot_general(
                d_ref[f + k], w_ref[k * width : (k + 1) * width, :], NT, preferred_element_type=F32
            )
        out_ref[f] = total.astype(BF16)
        for c in range(batch):
            one = copy(out_ref.at[f, pl.ds(c * sites, sites)], out_hbm.at[c, f], out_sem.at[f, c])
            one.start()
            sent.append(one)
    for one in kept + sent:
        one.wait()


def moments(first, second, grad):
    return 0.9 * first + 0.1 * grad, 0.99 * second + 0.01 * grad * grad


def stepped(weight, first_out, second_out):
    return (weight - 0.001 * first_out / (jnp.sqrt(second_out) + 1e-08)).astype(BF16)


def block_kernel(me_ref, parts_ref, mh_ref, vh_ref, wh_ref, send_ref):
    me = me_ref[0]
    half = me % 2
    slot = (me // 64) * 2 + (me // 4) % 2
    z_low = (me // 8) % 2
    _, block, width = parts_ref.shape
    rows = pl.ds(pl.multiple_of(slot * block, block), block)
    grad = jnp.sum(parts_ref[...].astype(F32), axis=0).astype(BF16)
    first = jnp.where(z_low == 0, mh_ref[rows, :width], mh_ref[rows, width:])
    second = jnp.where(z_low == 0, vh_ref[rows, :width], vh_ref[rows, width:])
    first_out, second_out = moments(first, second, grad.astype(F32))
    weight = jnp.where(z_low == 0, wh_ref[rows, :width].astype(F32), wh_ref[rows, width:].astype(F32))
    new = stepped(weight, first_out, second_out)
    for d in range(0, send_ref.shape[0], 2):
        send_ref[d + half] = grad
        send_ref[d + 1 - half] = new


def final_kernel(side, me_ref, blocks_ref, mh_ref, vh_ref, w_ref, *refs):
    half = me_ref[0] % 2
    core = (me_ref[0] // 2) % 2
    owner = core if side == 0 else 1 - core
    count, block, part_width = blocks_ref.shape
    slots = count // 2
    side_rows = mh_ref.shape[0]
    owned = 2 * side_rows
    start = pl.multiple_of(owner * side_rows, side_rows)
    pending = []
    if side == 0:
        m_hbm, v_hbm, w_hbm, new_hbm, first_hbm, second_hbm, m_next, v_next, w_next = refs[:9]
        new_ref, first_ref, second_ref, sem, other_sem, w_sem = refs[9:]
        other = pl.ds(pl.multiple_of((1 - owner) * side_rows, side_rows), side_rows)
        other_w = pl.ds(pl.multiple_of(half * owned + (1 - owner) * side_rows, side_rows), side_rows)
        pending = [
            copy(m_hbm.at[other], m_next, w_sem.at[0]),
            copy(v_hbm.at[other], v_next, w_sem.at[1]),
            copy(w_hbm.at[other_w], w_next, w_sem.at[2]),
        ]
        for one in pending:
            one.start()
    else:
        new_hbm, first_hbm, second_hbm, new_ref, first_ref, second_ref, sem, other_sem = refs[3:]
    sent = []
    for slot in range(slots // 2):
        peer = pl.ds(pl.multiple_of((1 - half) * owned + start + slot * block, block), block)
        for z in range(2):
            source = blocks_ref.at[(slot // 2) * 8 + z * 4 + (slot % 2) * 2 + 1 - half]
            cols = pl.ds(z * part_width, part_width)
            sent.append(copy(source, new_hbm.at[peer, cols], other_sem.at[slot, z]))
            sent[-1].start()
    per = 2
    rows = per * block
    chunks = slots // 2 // per

    def first_part(chunk):
        for slot in range(chunk * per, (chunk + 1) * per):
            here = slice(slot * block, (slot + 1) * block)
            index = (slot // 2) * 8 + (slot % 2) * 2 + half
            grad = jnp.concatenate([blocks_ref[index], blocks_ref[index + 4]], axis=1).astype(F32)
            first_out, second_out = moments(mh_ref[here, :], vh_ref[here, :], grad)
            first_ref[here, :] = first_out
            second_ref[here, :] = second_out
            new_ref[here, :] = stepped(w_ref[here, :].astype(F32), first_out, second_out)
        far = pl.ds(pl.multiple_of(start + chunk * rows, rows), rows)
        for i, (source, target) in enumerate([(first_ref, first_hbm), (second_ref, second_hbm)]):
            one = copy(source.at[pl.ds(chunk * rows, rows)], target.at[far], sem.at[chunk, i])
            one.start()
            sent.append(one)

    def second_part(chunk):
        mine = pl.ds(pl.multiple_of(half * owned + start + chunk * rows, rows), rows)
        one = copy(new_ref.at[pl.ds(chunk * rows, rows)], new_hbm.at[mine], sem.at[chunk, 2])
        one.start()
        sent.append(one)

    for chunk in range(chunks):
        first_part(chunk)
        second_part(chunk)
    for one in sent + pending:
        one.wait()


SCALAR = pl.BlockSpec(memory_space=pltpu.SMEM)
NEAR = pl.BlockSpec(memory_space=pltpu.VMEM)
FAR = pl.BlockSpec(memory_space=pltpu.HBM)
DMA = pltpu.SemaphoreType.DMA
PARAMS = pltpu.CompilerParams(vmem_limit_bytes=32 * 1024 * 1024)


def local(value):
    return pltpu.with_memory_space_constraint(value, pltpu.VMEM)


def remote(value):
    return pltpu.with_memory_space_constraint(value, pltpu.HBM)


def run_forward(me, clips, weight, proj, gain, code_bias, rotation, cotangent, devices):
    batch, frames, sites, width = clips.shape
    tokens = batch * sites
    rows = (frames, ROWS, tokens)
    outs = [
        pltpu.VMEM((frames, tokens, width), BF16), pltpu.VMEM(rows, F32), pltpu.VMEM((frames, 8, tokens), F32),
        pltpu.VMEM((ROWS, LANES), F32), pltpu.VMEM(rows, F32),
        pltpu.VMEM((2 * ROWS, width), BF16), pltpu.VMEM((devices, LANES), F32),
    ]
    return pl.pallas_call(
        forward_kernel,
        in_specs=[SCALAR] + [FAR] * 7,
        out_specs=[NEAR] * 7,
        out_shape=outs,
        scratch_shapes=[
            pltpu.VMEM((frames, tokens, width), BF16), pltpu.VMEM(weight.shape, BF16),
            pltpu.VMEM((ROWS, width), F32),
            *[pltpu.VMEM(a.shape, a.dtype) for a in (proj, gain, code_bias, rotation, cotangent)],
            DMA((frames, batch)), DMA((3,)), DMA((5,)),
        ],
        compiler_params=PARAMS,
        name="forward",
    )(me, *[remote(a) for a in (clips, weight, proj, gain, code_bias, rotation, cotangent)])


def run_window(clips, hidden, raw, inv, bias, cot):
    batch, frames, sites, width = clips.shape
    tokens = batch * sites
    return pl.pallas_call(
        window_kernel,
        in_specs=[FAR] + [NEAR] * 5,
        out_specs=[FAR] * 3,
        out_shape=[
            pltpu.HBM(hidden.shape, BF16), pltpu.HBM((width, frames * tokens), BF16),
            pltpu.HBM((frames, 3, *raw.shape[1:]), F32),
        ],
        scratch_shapes=[
            pltpu.VMEM((frames, tokens, width), BF16), pltpu.VMEM((width, frames * tokens), BF16),
            pltpu.VMEM((frames, 3, *raw.shape[1:]), F32), DMA((frames, batch)), DMA(()), DMA(()), DMA(()),
        ],
        compiler_params=PARAMS,
        name="window",
    )(remote(clips), *[local(a) for a in (hidden, raw, inv, bias, cot)])


def run_backward(bits, clip_count, token_count, me, saved, ag, parts, row_count):
    width = saved[0].shape[2]
    both = (2, 32, row_count // 32, width // 2)
    return pl.pallas_call(
        functools.partial(backward_kernel, bits, clip_count, token_count),
        in_specs=[SCALAR] + [FAR] * 3 + [NEAR] * 2,
        out_specs=[FAR] + [NEAR] * 2,
        out_shape=[
            pltpu.HBM(saved[0].shape, BF16), pltpu.VMEM(both, BF16),
            jax.ShapeDtypeStruct((1, 1), F32),
        ],
        scratch_shapes=[
            pltpu.VMEM((LANES, width), BF16), pltpu.VMEM(saved[1].shape, BF16), pltpu.VMEM(saved[0].shape, BF16),
            pltpu.VMEM((row_count, width), BF16), pltpu.VMEM(saved[0].shape, BF16),
            pltpu.VMEM(saved[2].shape, F32),
            DMA(()), *[DMA((saved[0].shape[0],))] * 3,
        ],
        compiler_params=PARAMS,
        name="backward",
    )(me, *[remote(a) for a in saved], local(ag), local(parts))


def run_input(me, d_conv, weight, first, second, shape):
    batch, frames = shape[:2]
    owned = (first.shape[0] // 2, first.shape[1])
    return pl.pallas_call(
        input_kernel,
        in_specs=[SCALAR] + [FAR] * 4,
        out_specs=[FAR, NEAR, NEAR, NEAR],
        out_shape=[
            pltpu.HBM(shape, BF16),
            pltpu.VMEM(owned, F32), pltpu.VMEM(owned, F32), pltpu.VMEM(owned, BF16),
        ],
        scratch_shapes=[
            pltpu.VMEM(weight.shape, BF16), pltpu.VMEM(d_conv.shape, BF16), pltpu.VMEM(d_conv.shape, BF16),
            DMA((3,)), DMA((3,)), DMA((frames, batch)), DMA((frames,)),
        ],
        compiler_params=PARAMS,
        name="input_grad",
    )(me, *[remote(a) for a in (d_conv, weight, first, second)])


def run_block(me, parts, kept):
    send = (32, *parts.shape[1:])
    return pl.pallas_call(
        block_kernel,
        in_specs=[SCALAR] + [NEAR] * 4,
        out_specs=NEAR,
        out_shape=pltpu.VMEM(send, BF16),
        compiler_params=PARAMS,
        name="owner_step",
    )(me, local(parts), *[local(a) for a in kept])


def run_near(me, blocks, weight, first, second, kept):
    owned, width = first.shape
    half = (owned // 2, width)
    return pl.pallas_call(
        functools.partial(final_kernel, 0),
        in_specs=[SCALAR] + [NEAR] * 4 + [FAR] * 3,
        out_specs=[FAR] * 3 + [NEAR] * 3,
        out_shape=[
            pltpu.HBM(weight.shape, BF16), pltpu.HBM(first.shape, F32), pltpu.HBM(first.shape, F32),
            pltpu.VMEM(half, F32), pltpu.VMEM(half, F32), pltpu.VMEM(half, BF16),
        ],
        scratch_shapes=[
            pltpu.VMEM(half, BF16), pltpu.VMEM(half, F32), pltpu.VMEM(half, F32),
            DMA((4, 3)), DMA((8, 2)), DMA((3,)),
        ],
        compiler_params=PARAMS,
        name="final_near",
    )(me, *[local(a) for a in (blocks, *kept)], *[remote(a) for a in (first, second, weight)])


def run_far(me, blocks, saved, carried):
    half = saved[0].shape
    return pl.pallas_call(
        functools.partial(final_kernel, 1),
        in_specs=[SCALAR] + [NEAR] * 4 + [FAR] * 3,
        out_specs=[FAR] * 3,
        out_shape=[pltpu.HBM(a.shape, a.dtype) for a in carried],
        scratch_shapes=[
            pltpu.VMEM(half, BF16), pltpu.VMEM(half, F32), pltpu.VMEM(half, F32), DMA((4, 3)), DMA((8, 2)),
        ],
        input_output_aliases={5 + i: i for i in range(3)},
        compiler_params=PARAMS,
        name="final_far",
    )(me, *[local(a) for a in (blocks, *saved)], *[remote(a) for a in carried])


def spread(value, axes):
    return lax.all_to_all(value, axes, 0, 0, tiled=True)


def swapped(value):
    return lax.ppermute(value, "core", [(0, 1), (1, 0)])


def on_device(clips, code_grad, conv_weight, norm_gain, proj_weight, code_bias, rotation, first_moment, second_moment):
    bits = code_grad.shape[3]
    devices = lax.axis_size(ALL)
    batch, frames, sites, width = clips.shape
    clip_count = batch * devices
    token_count = clip_count * frames * sites
    me = lax.axis_index(ALL).astype(jnp.int32).reshape(1)
    cotangent = code_grad.transpose(1, 3, 0, 2)
    hidden, raw, inv, bias, cot, ag, stats = run_forward(
        me, clips, conv_weight, proj_weight.T, norm_gain[None, :], code_bias[None, :], rotation, cotangent, devices
    )
    parts = spread(stats, ALL)
    saved = run_window(clips, hidden, raw, inv, bias, cot)
    d_conv, both, loss = run_backward(
        bits, clip_count, token_count, me, saved, ag, parts, conv_weight.shape[0]
    )
    chip = (both[0].astype(F32) + swapped(both[1]).astype(F32)).astype(BF16)
    plane = spread(chip, PLANE)
    input_grad, *kept = run_input(me, d_conv, conv_weight, first_moment, second_moment, clips.shape)
    plane, kept = lax.optimization_barrier((plane, kept))
    column = jnp.sum(plane.astype(F32), axis=0).astype(BF16)
    tower = spread(jnp.broadcast_to(column, (lax.axis_size("zh"), *column.shape)), "zh")
    near = spread(run_block(me, tower, kept), PLANE)
    far = swapped(near)
    outs = run_near(me, near, conv_weight, first_moment, second_moment, kept)
    new_weight, first_out, second_out = run_far(me, far, outs[3:], outs[:3])
    return new_weight, first_out, second_out, input_grad, loss[0, 0]


def solution(mesh):
    finer = Mesh(mesh.devices.reshape(4, 4, 2, 2, 2, mesh.shape["shard"]), ALL)
    split = P(ALL, None, None, None)
    in_specs = (split, split, P(), P(), P(), P(), P(), P("yl", None), P("yl", None))
    out_specs = (P(), P("yl", None), P("yl", None), split, P())
    return jax.shard_map(on_device, mesh=finer, in_specs=in_specs, out_specs=out_specs, check_vma=False)
```
